256 devices in a mesh: ctx: 16 (over y, x_lo, core), rep: 8 (over z), head: 2 (over x_hi).
Axes of the slice: x: 4 (x_hi: 2, x_lo: 2; x = x_hi * 2 + x_lo), y: 4, z: 8, core: 2. Of those that a mesh axis runs over, the one named last changes fastest.
Arguments:
- inputs: bfloat16 [8, 8192, 2048], P('rep', 'ctx', 'head'), may hold values from -6 to 6
- queries: bfloat16 [8, 8192, 2048], P('rep', 'ctx', 'head'), may hold values from -6 to 6
- keys: bfloat16 [8, 8192, 2048], P('rep', 'ctx', 'head'), may hold values from -6 to 6
- targets: bfloat16 [8, 8192, 2048], P('rep', 'ctx', 'head'), may hold values from -3 to 3
- value_weight: bfloat16 [8, 2048, 2048], P('rep', None, 'head'), may hold values from -0.125 to 0.125
- anchor: float32 [2048, 2048], P('ctx', 'head'), may hold values from -0.125 to 0.125
- momentum: float32 [2048, 2048], P('ctx', 'head'), may hold values from -6 to 6
Outputs:
- anchor_next: float32 [8, 2048, 2048], P('rep', 'ctx', 'head')
- momentum_next: float32 [8, 2048, 2048], P('rep', 'ctx', 'head')
The draws below stay inside these ranges and needn't reach their ends.
All inputs are finite; a program needn't handle non-finite values.
Results may differ from the reference program's by a relative error of at most 0.02.
Values may be sent and summed in bfloat16 or wider, within the bound.
A program may use at most 64 MiB of HBM per device.

```python
import jax
import jax.numpy as jnp
from jax import lax

D = 2048
HEAD_DIM = 128
TOK_DEV = 512
HEADS = 16
HEAD_WIDTH = 2048
SEQ = 8192
REPLICAS = 8
N_CTX = 16


def raised(values, stream_key, source, target, parts, factor):
    owner, partner = [(jnp.arange(values.shape[axis_at]) // (values.shape[axis_at] // parts)).reshape([-1 if axis == axis_at else 1 for axis in range(values.ndim)]) for axis_at in (source, target)]
    chosen = jax.random.permutation(stream_key, parts)[partner]
    strong = (owner == chosen) | (owner == (partner + parts // 2) % parts)
    return jnp.where(strong, factor * values, values)


def block_levels(key, shape, pieces, smallest, high):
    gain, own = 1.0, jax.random.fold_in(key, 6)
    for dim, shards_of in pieces:
        steps = jnp.exp(jax.random.uniform(jax.random.fold_in(own, dim), (shards_of,), jnp.float32, smallest / len(pieces), high / len(pieces)))
        gain = gain * jnp.repeat(steps, shape[dim] // shards_of).reshape([-1 if axis == dim else 1 for axis in range(len(shape))])
    return gain


def scatter_about(stream_key, dims, spread, reach, shards=(), held_as=jnp.bfloat16):
    values = spread * jax.random.normal(stream_key, dims, jnp.float32)
    if shards:
        values = values * block_levels(stream_key, dims, shards, -0.22, 0.18)
    return jnp.clip(values, -reach, reach).astype(held_as)


def bell_draw_with(own_key, extent, width, reach, pieces, heavy, held_as=jnp.bfloat16):
    entries = width * jax.random.normal(own_key, extent, jnp.float32)
    if pieces:
        entries = entries * block_levels(own_key, extent, pieces, -0.22, 0.18)
    return jnp.clip(raised(entries, jax.random.fold_in(own_key, 3), *heavy), -reach, reach).astype(held_as)


def setup_inputs(seed: int = 0) -> dict:
    splits = jax.random.split(jax.random.key(seed), 8)
    return {
        "inputs": bell_draw_with(splits[0], (REPLICAS, SEQ, D), 1.0, 6.0, ((0, 8), (1, 16), (2, 2)), (1, 2, 16, 2.0)),
        "queries": scatter_about(splits[1], (REPLICAS, SEQ, HEAD_WIDTH), 1.0, 6.0, ((0, 8), (1, 16), (2, 2))),
        "keys": scatter_about(splits[2], (REPLICAS, SEQ, HEAD_WIDTH), 1.0, 6.0, ((0, 8), (1, 16), (2, 2))),
        "targets": scatter_about(splits[3], (REPLICAS, SEQ, HEAD_WIDTH), 0.5, 3.0, ((0, 8), (1, 16), (2, 2))),
        "value_weight": scatter_about(splits[4], (REPLICAS, D, HEAD_WIDTH), D ** -0.5, 0.125, ((0, 8), (2, 2))),
        "anchor": scatter_about(splits[5], (D, HEAD_WIDTH), D ** -0.5, 0.125, ((0, 16), (1, 2)), jnp.float32),
        "momentum": scatter_about(splits[6], (D, HEAD_WIDTH), 1.0, 6.0, ((0, 16), (1, 2)), jnp.float32),
    }


inner_rate = 0.05
slow_decay = 0.5
outer_rate = 1.0

def reference(inputs, queries, keys, targets, value_weight, anchor, momentum):
    attn_scale = 1.0 / jnp.sqrt(jnp.float32(HEAD_DIM * SEQ))
    loss_scale = 1.0 / jnp.sqrt(jnp.float32(SEQ))
    causal = jnp.arange(TOK_DEV)[:, None] >= jnp.arange(TOK_DEV)[None, :]

    def blocks(array):
        return array.reshape(N_CTX, TOK_DEV, HEADS, HEAD_DIM)

    def masked(query_block, key_block):
        scores = jnp.einsum('thd,shd->hts', query_block.astype(jnp.float32), key_block.astype(jnp.float32))
        return lax.optimization_barrier(jnp.where(causal[None], scores, 0.0).astype(jnp.bfloat16)).astype(jnp.float32)

    def one_replica(packed):
        features, query_all, key_all, target_all, weights = packed
        values = jnp.dot(features, weights, preferred_element_type=jnp.float32).astype(jnp.bfloat16)
        query_blocks = blocks(query_all)
        key_blocks = blocks(key_all)
        value_blocks = blocks(values)

        def forward_block(state, block):
            query_block, key_block, value_block = block
            weighted = masked(query_block, key_block)
            rounded = lax.optimization_barrier(state.astype(jnp.bfloat16)).astype(jnp.float32)
            result = attn_scale * (jnp.einsum('hts,she->the', weighted, value_block.astype(jnp.float32)) + jnp.einsum('thd,hde->the', query_block.astype(jnp.float32), rounded))
            state = state + jnp.einsum('shd,she->hde', key_block.astype(jnp.float32), value_block.astype(jnp.float32))
            return (state, result)
        zeros = jnp.zeros((HEADS, HEAD_DIM, HEAD_DIM), jnp.float32)
        unused, outputs = lax.scan(forward_block, zeros, (query_blocks, key_blocks, value_blocks))
        grad_out = (loss_scale * (outputs - blocks(target_all).astype(jnp.float32))).astype(jnp.bfloat16)
        feature_blocks = features.reshape(N_CTX, TOK_DEV, D)

        def backward_block(carry, block):
            state, total = carry
            query_block, key_block, feature_block, grad_block = block
            weighted = masked(query_block, key_block)
            rounded = lax.optimization_barrier(state.astype(jnp.bfloat16)).astype(jnp.float32)
            grad_f32 = grad_block.astype(jnp.float32)
            grad_values = attn_scale * (jnp.einsum('hts,the->she', weighted, grad_f32) + jnp.einsum('shd,hde->she', key_block.astype(jnp.float32), rounded))
            grad_values = grad_values.astype(jnp.bfloat16).reshape(TOK_DEV, HEAD_WIDTH)
            term = jnp.dot(feature_block.T, grad_values, preferred_element_type=jnp.float32)
            term = lax.optimization_barrier(term.astype(jnp.bfloat16)).astype(jnp.float32)
            state = state + jnp.einsum('thd,the->hde', query_block.astype(jnp.float32), grad_f32)
            return ((state, total + term), None)
        start = (zeros, jnp.zeros((D, HEAD_WIDTH), jnp.float32))
        (unused_state, gradient), unused_out = lax.scan(backward_block, start, (query_blocks, key_blocks, feature_blocks, grad_out), reverse=True)
        return (anchor - weights.astype(jnp.float32)) / inner_rate + gradient
    deltas = lax.map(one_replica, (inputs, queries, keys, targets, value_weight))
    grouped = deltas.reshape(REPLICAS // 4, 4, D, HEAD_WIDTH)
    mixed = jnp.broadcast_to(lax.optimization_barrier(jnp.mean(grouped, axis=1, keepdims=True)), grouped.shape).reshape(REPLICAS, D, HEAD_WIDTH)
    momentum_next = slow_decay * momentum[None] + mixed
    anchor_next = anchor[None] - outer_rate * inner_rate * momentum_next
    return (anchor_next, momentum_next)
```

```python
import functools
import math

import jax
import jax.numpy as jnp
from jax import lax
from jax.experimental import pallas as pl
from jax.experimental.pallas import tpu as pltpu
from jax.sharding import PartitionSpec as P

HEAD_DIM = 128
GROUPS = 4
CHUNKS = 4
MESH = pl.DeviceIdType.MESH

inner_rate = 0.05
slow_decay = 0.5
outer_rate = 1.0

F32 = jnp.float32
BF16 = jnp.bfloat16


def dot(a, b):
    return jnp.dot(a, b, preferred_element_type=F32)


def lanes(index, size=HEAD_DIM):
    return pl.ds(pl.multiple_of(index * size, size), size)


def kernel(
    attn_scale,
    loss_scale,
    x_ref,
    q_ref,
    k_ref,
    t_ref,
    w_ref,
    a_ref,
    out_ref,
    x2,
    xp,
    xt,
    rel,
    qv,
    kv,
    tv,
    wv,
    av,
    qt,
    kt,
    sc,
    sct,
    wqk,
    vp,
    vv,
    gl,
    base,
    st,
    cr,
    tt,
    yr,
    xs,
    xr,
    ps,
    pr,
    gv,
    s1,
    r1,
    s2,
    r2,
    own,
    sx,
    rx,
    dz,
    rz,
    mz,
    mixb,
    load_sem,
    f_send,
    f_recv,
    p_send,
    p_recv,
    c_send,
    c_recv,
    y_send,
    y_recv,
    x_send,
    x_recv,
    b_send,
    b_recv,
    g_send,
    g_recv,
    r1_send,
    r1_recv,
    r2_send,
    r2_recv,
    rx_send,
    rx_recv,
    rz_send,
    rz_recv,
    mz_send,
    mz_recv,
):
    tokens, width = qv.shape
    half = x2.shape[2]
    heads = width // HEAD_DIM
    per_group = heads // GROUPS
    mine = per_group // 2
    cols = per_group * HEAD_DIM
    rows_dev = av.shape[0]
    gc = loss_scale * attn_scale

    me = lax.axis_index("ctx")
    rep = lax.axis_index("rep")
    head = lax.axis_index("head")
    core = lax.rem(me, 2)
    xl = lax.rem(me // 2, 2)
    y = me // 4
    low = lax.rem(me, 4)
    core_peer = (me + 1 - 2 * core, rep, head)
    x_id = me + 2 - 4 * xl
    x_peer = (x_id, rep, head)
    far_peer = (x_id, rep, 1 - head)
    y_up = (lax.rem(y + 1, 4) * 4 + low, rep, head)
    y_down = (lax.rem(y + 3, 4) * 4 + low, rep, head)
    zk = lax.rem(rep, 4)
    z_ids = [lax.rem(zk + d, 4) for d in (1, 2, 3)]
    z_peers = [(me, rep - zk + z, head) for z in z_ids]

    def remote(src, dst, send, recv, peer):
        return pltpu.make_async_remote_copy(
            src_ref=src, dst_ref=dst, send_sem=send, recv_sem=recv, device_id=peer, device_id_type=MESH
        )

    own_rows = pl.ds(pl.multiple_of(head * half, half), half)
    other_rows = pl.ds(pl.multiple_of((1 - head) * half, half), half)
    loads = [
        pltpu.make_async_copy(src, dst, load_sem.at[n])
        for n, (src, dst) in enumerate(
            (
                (q_ref, qv),
                (k_ref, kv),
                (x_ref, x2.at[0]),
                (w_ref.at[own_rows], wv.at[0]),
                (t_ref, tv),
                (w_ref.at[other_rows], wv.at[1]),
                (w_ref.at[pl.ds(pl.multiple_of(me * rows_dev, rows_dev), rows_dev)], wv.at[2, pl.ds(0, rows_dev)]),
                (a_ref, av),
            )
        )
    ]
    for copy in loads:
        copy.start()

    yr[...] = jnp.zeros_like(yr)

    barrier = pltpu.get_barrier_semaphore()
    peers = [core_peer, x_peer, far_peer, y_up, y_down, *z_peers]
    for peer in peers:
        pl.semaphore_signal(barrier, inc=1, device_id=peer, device_id_type=MESH)

    pl.semaphore_wait(barrier, len(peers))

    piece = tokens // 2 // CHUNKS
    first = []
    for n in range(CHUNKS):
        for side, peer in ((0, x_peer), (1, far_peer)):
            at = side * (tokens // 2) + n * piece
            first.append(
                remote(x_ref.at[pl.ds(at, piece)], rel.at[side, n], f_send.at[side, n], f_recv.at[side, n], peer)
            )
            first[-1].start()
    swaps = []
    for n in range(4):
        src = x_ref.at[:, lanes(2 * n + 1 - core)]
        swaps.append(remote(src, xp.at[head * 4 + n], p_send.at[0, n], p_recv.at[0, n], core_peer))
        swaps[-1].start()

    second = []

    def relay(n):
        for side, peer in ((0, far_peer), (1, x_peer)):
            first[2 * n + side].wait_recv()
            at = side * (tokens // 2) + n * piece
            second.append(
                remote(
                    rel.at[side, n],
                    x2.at[1, pl.ds(at, piece)],
                    f_send.at[2 + side, n],
                    f_recv.at[2 + side, n],
                    peer,
                )
            )
            second[-1].start()

    loads[0].wait()
    loads[1].wait()
    mid = tokens // 2

    def scores(h, carry):
        at = lanes(h)
        q = qv[:, at]
        k = kv[:, at]
        q_t = q.T
        k_t = k.T
        qt[h] = q_t
        kt[h] = k_t
        row = lax.broadcasted_iota(jnp.int32, (mid, mid), 0)
        col = lax.broadcasted_iota(jnp.int32, (mid, mid), 1)
        lower = row >= col
        upper = row <= col
        for n in range(2):
            rows = slice(n * mid, (n + 1) * mid)
            sc[h, rows, rows] = jnp.where(lower, dot(q[rows], k_t[:, rows]), 0.0).astype(BF16)
            sct[h, rows, rows] = jnp.where(upper, dot(k[rows], q_t[:, rows]), 0.0).astype(BF16)
        sc[h, mid:, :mid] = dot(q[mid:], k_t[:, :mid]).astype(BF16)
        sct[h, :mid, mid:] = dot(k[:mid], q_t[:, mid:]).astype(BF16)
        wqk[h, :mid, :HEAD_DIM] = (gc * dot(sct[h, :mid, :], q)).astype(BF16)
        wqk[h, mid:, :HEAD_DIM] = (gc * dot(sct[h, mid:, mid:], q[mid:])).astype(BF16)
        wqk[h, :, HEAD_DIM:] = k
        st[0, h] = dot(q_t, q).astype(BF16)
        return carry

    lax.fori_loop(0, heads, scores, 0)

    pending = []

    def heads_of(g, which):
        return pl.ds(g * per_group + which * mine, mine)

    def scan_core(kind, g):
        copy = remote(
            st.at[kind, heads_of(g, 1 - core)], cr.at[kind, g], c_send.at[kind, g], c_recv.at[kind, g], core_peer
        )
        copy.start()
        pending.append(copy)

    def y_copy(kind, g, n, src, peer):
        return remote(src, yr.at[kind, n, g], y_send.at[kind, n, g], y_recv.at[kind, n, g], peer)

    def y_copies(kind, g):
        ahead, behind = (y_up, y_down) if kind == 1 else (y_down, y_up)
        return (
            y_copy(kind, g, 0, tt.at[kind, g], ahead),
            y_copy(kind, g, 1, yr.at[kind, 0, g], ahead),
            y_copy(kind, g, 2, tt.at[kind, g], behind),
        )

    def place(kind):
        return y if kind == 1 else 3 - y

    def scan_y(kind, g):
        remote(
            st.at[kind, heads_of(g, 1 - core)], cr.at[kind, g], c_send.at[kind, g], c_recv.at[kind, g], core_peer
        ).wait_recv()
        total = st[kind, heads_of(g, core)].astype(F32) + cr[kind, g].astype(F32)
        tt[kind, g] = total.astype(BF16)
        step, _, wrap = y_copies(kind, g)
        pl.when(place(kind) < 3)(step.start)
        pl.when(place(kind) == 0)(wrap.start)

    def scan_relay(kind, g):
        step, pass_on, _ = y_copies(kind, g)
        pl.when(place(kind) > 0)(step.wait_recv)
        pl.when((place(kind) == 1) | (place(kind) == 2))(pass_on.start)

    def x_copy(kind, g):
        return remote(xs.at[kind, g], xr.at[kind, g], x_send.at[kind, g], x_recv.at[kind, g], x_peer)

    def earlier(kind, g):
        return yr[kind, 0, g].astype(F32) + yr[kind, 1, g].astype(F32) + yr[kind, 2, g].astype(F32)

    def scan_x(kind, g):
        _, pass_on, wrap = y_copies(kind, g)
        pl.when(place(kind) > 1)(pass_on.wait_recv)
        pl.when(place(kind) == 3)(wrap.wait_recv)
        gives = (xl == 0) if kind == 1 else (xl == 1)
        sent = earlier(kind, g) + jnp.where(gives, tt[kind, g].astype(F32), 0.0)
        xs[kind, g] = sent.astype(BF16)
        copy = x_copy(kind, g)
        copy.start()
        pending.append(copy)

    def b_copy(kind, g):
        return remote(
            ps.at[kind, g], pr.at[kind, heads_of(g, core)], b_send.at[kind, g], b_recv.at[kind, g], core_peer
        )

    def scan_back(kind, g):
        x_copy(kind, g).wait_recv()
        chip = earlier(kind, g) + xr[kind, g].astype(F32)
        later = (core == 1) if kind == 1 else (core == 0)
        mine_too = st[kind, heads_of(g, core)].astype(F32)
        theirs = cr[kind, g].astype(F32)
        ps[kind, g] = jnp.where(later, chip, chip + mine_too).astype(BF16)
        pr[kind, heads_of(g, core)] = jnp.where(later, chip + theirs, chip).astype(BF16)
        copy = b_copy(kind, g)
        copy.start()
        pending.append(copy)

    def scan_end(kind, g):
        b_copy(kind, g).wait_recv()

    for g in range(GROUPS):
        scan_core(0, g)

    relay(0)
    relay(1)

    loads[2].wait()
    loads[3].wait()
    wide = 256

    def partial(n, carry):
        at = lanes(n, wide)
        vp[:, at] = dot(x2[0], wv[0, :, at])
        return carry

    lax.fori_loop(0, width // wide, partial, 0)

    for g in range(GROUPS):
        scan_y(0, g)
    relay(2)
    relay(3)

    def turn_own(side):
        def turn(n, carry):
            at = lanes(((head + side) % 2) * 4 + n)
            xt[at, :tokens] = x2[side, :, lanes(2 * n + core)].T
            return carry

        lax.fori_loop(0, 4, turn, 0)

    def turn_theirs(side):
        def turn(n, carry):
            block = ((head + side) % 2) * 4 + n
            xt[lanes(block), tokens:] = xp[block].T
            return carry

        lax.fori_loop(0, 4, turn, 0)

    turn_own(0)
    for g in range(GROUPS):
        scan_relay(0, g)
    for copy in swaps:
        copy.wait_recv()
    turn_theirs(0)
    loads[4].wait()
    loads[5].wait()
    for g in range(GROUPS):
        scan_x(0, g)

    def finish(n):
        for side in range(2):
            for m in (2 * n, 2 * n + 1):
                second[2 * m + side].wait_recv()
        size = 2 * piece

        def values(m, carry):
            at = lanes(m, wide)
            for side in range(2):
                rows = slice(side * mid + n * size, side * mid + (n + 1) * size)
                vv[rows, at] = (vp[rows, at] + dot(x2[1, rows, :], wv[1, :, at])).astype(BF16)
            return carry

        lax.fori_loop(0, width // wide, values, 0)

    finish(0)
    finish(1)
    for n in range(4):
        src = x2.at[1, :, lanes(2 * n + 1 - core)]
        swaps.append(remote(src, xp.at[(1 - head) * 4 + n], p_send.at[1, n], p_recv.at[1, n], core_peer))
        swaps[-1].start()
    for g in range(GROUPS):
        scan_back(0, g)
    for g in range(GROUPS):
        scan_end(0, g)

    def states(h, carry):
        at = lanes(h)
        v = vv[:, at]
        state = dot(kt[h], v).astype(BF16)
        st[1, h] = state
        top = dot(sc[h, :mid, :mid], v[:mid])
        bottom = dot(sc[h, mid:, :], v)
        scaled = loss_scale * attn_scale
        gl[:mid, at] = (scaled * top - loss_scale * tv[:mid, at].astype(F32)).astype(BF16)
        gl[mid:, at] = (scaled * bottom - loss_scale * tv[mid:, at].astype(F32)).astype(BF16)
        st[2, h] = (dot(qt[h], gl[:, at]) + gc * dot(pr[0, h], state)).astype(BF16)
        return carry

    def bases(h, carry):
        at = lanes(h)
        base[:mid, at] = dot(sct[h, :mid, :], gl[:, at])
        base[mid:, at] = dot(sct[h, mid:, mid:], gl[mid:, at])
        return carry

    def over(body, g):
        lax.fori_loop(g * per_group, (g + 1) * per_group, body, 0)

    def gv_copy(g):
        return remote(gv.at[g, pl.ds(0, tokens)], gv.at[g, pl.ds(tokens, tokens)], g_send.at[g], g_recv.at[g], core_peer)

    def grads(g):
        def one(n, carry):
            h = g * per_group + n
            at = lanes(h)
            prefix = pr[1, h]
            both = (prefix.astype(F32) + st[1, h].astype(F32)).astype(BF16)
            suffix = (gc * dot(pr[0, h], both) + pr[2, h].astype(F32)).astype(BF16)
            pair = jnp.concatenate([prefix, suffix], axis=0)
            gv[g, :tokens, lanes(n)] = (attn_scale * (base[:, at] + dot(wqk[h], pair))).astype(BF16)
            return carry

        lax.fori_loop(0, per_group, one, 0)
        copy = gv_copy(g)
        copy.start()
        pending.append(copy)

    two = 2 * rows_dev
    part = cols // 2

    def block(g, to):
        return dot(xt[pl.ds(pl.multiple_of(to * two, two), two), :], gv[g])

    def r1_copies(g):
        return (
            remote(s1.at[g, 0], r1.at[g, 0], r1_send.at[g, 0], r1_recv.at[g, 0], y_up),
            remote(s1.at[g, 1], r1.at[g, 1], r1_send.at[g, 1], r1_recv.at[g, 1], y_down),
        )

    def r2_copies(g):
        return (
            remote(s2.at[g, 0], r2.at[g, 0], r2_send.at[g, 0], r2_recv.at[g, 0], y_up),
            remote(s2.at[g, 1], r2.at[g, 1], r2_send.at[g, 1], r2_recv.at[g, 1], y_down),
        )

    def reduce_one(g):
        gv_copy(g).wait_recv()
        across = block(g, lax.rem(y + 2, 4)).astype(BF16)
        s1[g, 0] = across[:, :part]
        s1[g, 1] = across[:, part:]
        for copy in r1_copies(g):
            copy.start()
            pending.append(copy)

    def reduce_two(g):
        up = block(g, lax.rem(y + 1, 4))
        down = block(g, lax.rem(y + 3, 4))
        one = r1_copies(g)
        s2[g, 0, :, part:] = up[:, part:].astype(BF16)
        s2[g, 1, :, :part] = down[:, :part].astype(BF16)
        one[0].wait_recv()
        s2[g, 0, :, :part] = (up[:, :part] + r1[g, 0].astype(F32)).astype(BF16)
        one[1].wait_recv()
        s2[g, 1, :, part:] = (down[:, part:] + r1[g, 1].astype(F32)).astype(BF16)
        for copy in r2_copies(g):
            copy.start()
            pending.append(copy)
        own[g] = block(g, y)

    def rx_copy(g):
        return remote(sx.at[g], rx.at[g], rx_send.at[g], rx_recv.at[g], x_peer)

    def block_rows(which):
        return pl.ds(pl.multiple_of(which * rows_dev, rows_dev), rows_dev)

    def reduce_x(g):
        for copy in r2_copies(g):
            copy.wait_recv()
        rows = block_rows(1 - xl)
        sx[g] = (own[g, rows, :] + r2[g, 0, rows, :].astype(F32) + r2[g, 1, rows, :].astype(F32)).astype(BF16)
        copy = rx_copy(g)
        copy.start()
        pending.append(copy)

    share = rows_dev // 4

    def piece_rows(which):
        return pl.ds(pl.multiple_of(which * share, share), share)

    def rz_copies(g):
        return [
            remote(dz.at[g, piece_rows(z)], rz.at[g, n], rz_send.at[g, n], rz_recv.at[g, n], peer)
            for n, (z, peer) in enumerate(zip(z_ids, z_peers))
        ]

    def reduce_z(g):
        rx_copy(g).wait_recv()
        rows = block_rows(xl)
        at = slice(g * cols, (g + 1) * cols)
        total = own[g, rows, :] + r2[g, 0, rows, :].astype(F32) + r2[g, 1, rows, :].astype(F32)
        drift = (av[:, at] - wv[2, :rows_dev, at].astype(F32)) / inner_rate
        dz[g] = (total + rx[g].astype(F32) + drift).astype(BF16)
        for copy in rz_copies(g):
            copy.start()
            pending.append(copy)

    def mz_copies(g):
        at = slice(g * cols, (g + 1) * cols)
        return [
            remote(mz.at[g], mixb.at[piece_rows(zk), at], mz_send.at[g, n], mz_recv.at[g, n], peer)
            for n, peer in enumerate(z_peers)
        ]

    def mix(g):
        for copy in rz_copies(g):
            copy.wait_recv()
        at = slice(g * cols, (g + 1) * cols)
        total = dz[g, piece_rows(zk), :].astype(F32)
        for n in range(3):
            total += rz[g, n].astype(F32)
        mean = (0.25 * total).astype(BF16)
        mz[g] = mean
        mixb[piece_rows(zk), at] = mean
        for copy in mz_copies(g):
            copy.start()
            pending.append(copy)

    def settle(g):
        for copy in mz_copies(g):
            copy.wait_recv()

    kinds = (1, 2)

    def each(stage):
        def run(g):
            for kind in kinds:
                stage(kind, g)

        return run

    loads[6].wait()
    loads[7].wait()

    def start_group(g):
        over(states, g)
        for kind in kinds:
            scan_core(kind, g)

    def prepare():
        turn_own(1)
        for copy in swaps[4:]:
            copy.wait_recv()
        turn_theirs(1)

    def end_group(g):
        for kind in kinds:
            scan_end(kind, g)
        grads(g)

    stages = [
        start_group,
        each(scan_y),
        each(scan_relay),
        each(scan_x),
        each(scan_back),
        end_group,
        reduce_one,
        reduce_two,
        reduce_x,
        reduce_z,
        mix,
        settle,
    ]
    for turn in range(GROUPS + len(stages) - 1):
        for n in range(len(stages) - 1, -1, -1):
            g = turn - n
            if 0 <= g < GROUPS:
                stages[n](g)
        if turn < GROUPS:
            over(bases, turn)
        if turn == GROUPS - 1:
            prepare()

    out_ref[...] = mixb[...].astype(F32)

    for copy in first + second + swaps + pending:
        copy.wait_send()
    for kind in range(3):
        for g in range(GROUPS):
            step, pass_on, wrap = y_copies(kind, g)
            pl.when(place(kind) < 3)(step.wait_send)
            pl.when((place(kind) == 1) | (place(kind) == 2))(pass_on.wait_send)
            pl.when(place(kind) == 0)(wrap.wait_send)


def mixed_delta(x, q, k, t, w, a, attn_scale, loss_scale):
    tokens, half = x.shape
    width = q.shape[1]
    heads = width // HEAD_DIM
    rows_dev = a.shape[0]
    groups = GROUPS
    per_group = heads // groups
    mine = per_group // 2
    cols = per_group * HEAD_DIM
    two = 2 * rows_dev
    piece = tokens // 2 // CHUNKS
    state = (HEAD_DIM, HEAD_DIM)
    vmem = pltpu.VMEM
    dma = pltpu.SemaphoreType.DMA
    scratch = [
        vmem((2, tokens, half), BF16),
        vmem((8, tokens, HEAD_DIM), BF16),
        vmem((8 * HEAD_DIM, 2 * tokens), BF16),
        vmem((2, CHUNKS, piece, half), BF16),
        vmem((tokens, width), BF16),
        vmem((tokens, width), BF16),
        vmem((tokens, width), BF16),
        vmem((3, half, width), BF16),
        vmem((rows_dev, width), F32),
        vmem((heads, HEAD_DIM, tokens), BF16),
        vmem((heads, HEAD_DIM, tokens), BF16),
        vmem((heads, tokens, tokens), BF16),
        vmem((heads, tokens, tokens), BF16),
        vmem((heads, tokens, 2 * HEAD_DIM), BF16),
        vmem((tokens, width), F32),
        vmem((tokens, width), BF16),
        vmem((tokens, width), BF16),
        vmem((tokens, width), F32),
        vmem((3, heads, *state), BF16),
        vmem((3, groups, mine, *state), BF16),
        vmem((3, groups, mine, *state), BF16),
        vmem((3, 3, groups, mine, *state), BF16),
        vmem((3, groups, mine, *state), BF16),
        vmem((3, groups, mine, *state), BF16),
        vmem((3, groups, mine, *state), BF16),
        vmem((3, heads, *state), BF16),
        vmem((groups, 2 * tokens, cols), BF16),
        vmem((groups, 2, two, cols // 2), BF16),
        vmem((groups, 2, two, cols // 2), BF16),
        vmem((groups, 2, two, cols), BF16),
        vmem((groups, 2, two, cols), BF16),
        vmem((groups, two, cols), F32),
        vmem((groups, rows_dev, cols), BF16),
        vmem((groups, rows_dev, cols), BF16),
        vmem((groups, rows_dev, cols), BF16),
        vmem((groups, 3, rows_dev // 4, cols), BF16),
        vmem((groups, rows_dev // 4, cols), BF16),
        vmem((rows_dev, width), BF16),
        dma((8,)),
        dma((4, CHUNKS)),
        dma((4, CHUNKS)),
        dma((2, 4)),
        dma((2, 4)),
        dma((3, groups)),
        dma((3, groups)),
        dma((3, 3, groups)),
        dma((3, 3, groups)),
        dma((3, groups)),
        dma((3, groups)),
        dma((3, groups)),
        dma((3, groups)),
        dma((groups,)),
        dma((groups,)),
        dma((groups, 2)),
        dma((groups, 2)),
        dma((groups, 2)),
        dma((groups, 2)),
        dma((groups,)),
        dma((groups,)),
        dma((groups, 3)),
        dma((groups, 3)),
        dma((groups, 3)),
        dma((groups, 3)),
    ]
    return pl.pallas_call(
        functools.partial(kernel, attn_scale, loss_scale),
        out_shape=jax.ShapeDtypeStruct((rows_dev, width), F32),
        in_specs=[pl.BlockSpec(memory_space=pl.ANY)] * 6,
        out_specs=pl.BlockSpec(memory_space=pltpu.VMEM),
        scratch_shapes=scratch,
        compiler_params=pltpu.CompilerParams(
            collective_id=0, has_side_effects=True, vmem_limit_bytes=60 * 1024 * 1024
        ),
    )(x, q, k, t, w, a)


def local(inputs, queries, keys, targets, value_weight, anchor, momentum):
    sequence = queries.shape[1] * lax.axis_size("ctx")
    attn_scale = 1.0 / math.sqrt(HEAD_DIM * sequence)
    loss_scale = 1.0 / math.sqrt(sequence)
    mixed = mixed_delta(
        inputs[0], queries[0], keys[0], targets[0], value_weight[0], anchor, attn_scale, loss_scale
    )
    momentum_next = slow_decay * momentum + mixed
    anchor_next = anchor - outer_rate * inner_rate * momentum_next
    return (anchor_next[None], momentum_next[None])


def solution(mesh):
    placed = (
        P("rep", "ctx", "head"),
        P("rep", "ctx", "head"),
        P("rep", "ctx", "head"),
        P("rep", "ctx", "head"),
        P("rep", None, "head"),
        P("ctx", "head"),
        P("ctx", "head"),
    )
    return jax.shard_map(
        local,
        mesh=mesh,
        in_specs=placed,
        out_specs=(P("rep", "ctx", "head"), P("rep", "ctx", "head")),
        check_vma=False,
    )
```

```python
import functools
import math

import jax
import jax.numpy as jnp
from jax import lax
from jax.experimental import pallas as pl
from jax.experimental.pallas import tpu as pltpu
from jax.sharding import PartitionSpec as P

HEAD_DIM = 128
GROUPS = 4
CHUNKS = 4
MESH = pl.DeviceIdType.MESH

ORDER = (
    ("state", 0), ("later", 0), ("state", 1), ("a_rest", 0), ("y", 0), ("state", 2), ("later", 1), ("state", 3),
    ("later", 2), ("y", 1), ("later", 3), ("x", 0), ("base", 0), ("y", 2), ("base", 1), ("y", 3), ("x", 1),
    ("back", 0), ("prepare", 0), ("x", 2), ("know", 0), ("grad", 0), ("x", 3), ("back", 1), ("r1", 0), ("base", 2), ("sides", 0),
    ("grad", 1), ("back", 2), ("r1", 1), ("r2", 0), ("back", 3), ("base", 3), ("grad", 2), ("own", 0), ("sides", 1), ("r1", 2),
    ("r2", 1), ("grad", 3), ("rx", 0), ("r1", 3), ("sides", 2), ("r2", 2), ("own", 1), ("sides", 3), ("know_all", 0), ("rz", 0), ("r2", 3),
    ("rx", 1), ("own", 2), ("rz", 1), ("own", 3), ("rx", 2), ("mix", 0), ("rz", 2), ("mix", 1), ("rx", 3), ("rz", 3), ("end", 0), ("mix", 2), ("end", 1),
    ("mix", 3), ("end", 2), ("end", 3),
)

inner_rate = 0.05
slow_decay = 0.5
outer_rate = 1.0

F32 = jnp.float32
BF16 = jnp.bfloat16


def dot(a, b):
    return jnp.dot(a, b, preferred_element_type=F32)


def lanes(index, size=HEAD_DIM):
    return pl.ds(pl.multiple_of(index * size, size), size)


def kernel(
    attn_scale,
    loss_scale,
    x_ref,
    q_ref,
    k_ref,
    t_ref,
    w_ref,
    a_ref,
    out_ref,
    x2,
    xp,
    xt,
    rel,
    qv,
    kv,
    tv,
    wv,
    av,
    qt,
    kt,
    sc,
    sct,
    wqk,
    vp,
    vv,
    gl,
    base,
    st,
    cr,
    tt,
    yr,
    xs,
    xr,
    ps,
    pr,
    gv,
    keep,
    s1,
    r1,
    s2,
    r2,
    own,
    sx,
    rx,
    dz,
    rz,
    mz,
    mixb,
    uu,
    load_sem,
    sent,
    f_recv,
    p_recv,
    a_recv,
    ay_recv,
    c_recv,
    y_recv,
    x_recv,
    b_recv,
    g_recv,
    r1_recv,
    r2_recv,
    rx_recv,
    rz_recv,
    mz_recv,
    y_known,
    low_known,
    high_known,
):
    tokens, width = qv.shape
    half = x2.shape[2]
    heads = width // HEAD_DIM
    per_group = heads // GROUPS
    mine = per_group // 2
    cols = per_group * HEAD_DIM
    rows_dev = av.shape[0]
    gc = loss_scale * attn_scale

    me = lax.axis_index("ctx")
    rep = lax.axis_index("rep")
    head = lax.axis_index("head")
    core = lax.rem(me, 2)
    xl = lax.rem(me // 2, 2)
    y = me // 4
    low = lax.rem(me, 4)
    core_peer = (me + 1 - 2 * core, rep, head)
    x_id = me + 2 - 4 * xl
    x_peer = (x_id, rep, head)
    far_peer = (x_id, rep, 1 - head)
    y_up = (lax.rem(y + 1, 4) * 4 + low, rep, head)
    y_down = (lax.rem(y + 3, 4) * 4 + low, rep, head)
    zk = lax.rem(rep, 4)
    y_far = (lax.rem(y + 2, 4) * 4 + low, rep, head)
    z_up = (me, lax.rem(rep + 1, 8), head)
    z_down = (me, lax.rem(rep + 7, 8), head)
    z_ids = [lax.rem(zk + d, 4) for d in (1, 2, 3)]
    z_peers = [(me, rep - zk + z, head) for z in z_ids]

    def remote(src, dst, send, recv, peer):
        return pltpu.make_async_remote_copy(
            src_ref=src, dst_ref=dst, send_sem=send, recv_sem=recv, device_id=peer, device_id_type=MESH
        )

    own_rows = pl.ds(pl.multiple_of(head * half, half), half)
    other_rows = pl.ds(pl.multiple_of((1 - head) * half, half), half)
    loads = [
        pltpu.make_async_copy(src, dst, load_sem.at[n])
        for n, (src, dst) in enumerate(
            (
                (q_ref, qv),
                (k_ref, kv),
                (x_ref, x2.at[0]),
                (w_ref.at[own_rows], wv.at[0]),
                (t_ref, tv),
                (w_ref.at[other_rows], wv.at[1]),
                (w_ref.at[pl.ds(pl.multiple_of(me * rows_dev, rows_dev), rows_dev)], wv.at[2, pl.ds(0, rows_dev)]),
                (a_ref, av),
            )
        )
    ]
    for copy in loads:
        copy.start()

    yr[...] = jnp.zeros_like(yr)

    barrier = pltpu.get_barrier_semaphore()
    peers = [core_peer, x_peer, far_peer, y_up, y_down, z_up, z_down]
    for peer in peers:
        pl.semaphore_signal(barrier, inc=1, device_id=peer, device_id_type=MESH)

    pl.semaphore_wait(barrier, len(peers))

    def tell(sem, peer):
        pl.semaphore_signal(sem, inc=1, device_id=peer, device_id_type=MESH)

    piece = tokens // 2 // CHUNKS
    first = []
    for n in range(CHUNKS):
        for side, peer in ((0, x_peer), (1, far_peer)):
            at = side * (tokens // 2) + n * piece
            first.append(
                remote(x_ref.at[pl.ds(at, piece)], rel.at[side, n], sent.at[0], f_recv.at[side, n], peer)
            )
            first[-1].start()
    swaps = []
    for n in range(4):
        src = x_ref.at[:, lanes(2 * n + 1 - core)]
        swaps.append(remote(src, xp.at[head * 4 + n], sent.at[2], p_recv.at[0, n], core_peer))
        swaps[-1].start()

    tell(y_known, y_down)
    inner = (zk > 0) & (zk < 3)

    @pl.when(inner)
    def _():
        tell(low_known, z_down)
        tell(high_known, z_up)

    second = []

    def relay(n):
        for side, peer in ((0, far_peer), (1, x_peer)):
            first[2 * n + side].wait_recv()
            at = side * (tokens // 2) + n * piece
            second.append(
                remote(
                    rel.at[side, n],
                    x2.at[1, pl.ds(at, piece)],
                    sent.at[1],
                    f_recv.at[2 + side, n],
                    peer,
                )
            )
            second[-1].start()

    loads[0].wait()
    loads[1].wait()
    mid = tokens // 2

    def scores(h, carry):
        at = lanes(h)
        q = qv[:, at]
        k = kv[:, at]
        q_t = q.T
        k_t = k.T
        qt[h] = q_t
        kt[h] = k_t
        row = lax.broadcasted_iota(jnp.int32, (mid, mid), 0)
        col = lax.broadcasted_iota(jnp.int32, (mid, mid), 1)
        lower = row >= col
        upper = row <= col
        for n in range(2):
            rows = slice(n * mid, (n + 1) * mid)
            sc[h, rows, rows] = jnp.where(lower, dot(q[rows], k_t[:, rows]), 0.0).astype(BF16)
            sct[h, rows, rows] = jnp.where(upper, dot(k[rows], q_t[:, rows]), 0.0).astype(BF16)
        sc[h, mid:, :mid] = dot(q[mid:], k_t[:, :mid]).astype(BF16)
        sct[h, :mid, mid:] = dot(k[:mid], q_t[:, mid:]).astype(BF16)
        wqk[h, :mid, :HEAD_DIM] = (gc * dot(sct[h, :mid, :], q)).astype(BF16)
        wqk[h, mid:, :HEAD_DIM] = (gc * dot(sct[h, mid:, mid:], q[mid:])).astype(BF16)
        wqk[h, :, HEAD_DIM:] = k
        st[0, h // per_group, lax.rem(h, per_group) // mine, lax.rem(h, mine)] = dot(q_t, q).astype(BF16)
        return carry

    lax.fori_loop(0, heads, scores, 0)

    both = pl.ds(1, 2)
    alone = pl.ds(0, 1)

    def place(kind):
        return y if kind == 1 else 3 - y

    def core_copy(kinds, g, sem, recv):
        return remote(st.at[kinds, g, 1 - core], cr.at[kinds, g], sent.at[sem], recv, core_peer)

    def y_copies(kind, g, recv, sem):
        ahead, behind = (y_up, y_down) if kind == 1 else (y_down, y_up)
        return [
            remote(tt.at[kind, g], yr.at[kind, d, g], sent.at[sem + d], recv.at[d], peer)
            for d, peer in enumerate((ahead, y_far, behind))
        ]

    def y_send(kind, g, recv, sem):
        total = st[kind, g, core].astype(F32) + cr[kind, g].astype(F32)
        tt[kind, g] = total.astype(BF16)
        for d, copy in enumerate(y_copies(kind, g, recv, sem)):
            pl.when(place(kind) < 3 - d)(copy.start)

    def y_wait(kind, g, recv, sem):
        for d, copy in enumerate(y_copies(kind, g, recv, sem)):
            pl.when(place(kind) > d)(copy.wait_recv)

    def earlier(kind, g):
        return yr[kind, 0, g].astype(F32) + yr[kind, 1, g].astype(F32) + yr[kind, 2, g].astype(F32)

    def x_fill(kind, g):
        gives = (xl == 0) if kind == 1 else (xl == 1)
        xs[kind, g] = (earlier(kind, g) + jnp.where(gives, tt[kind, g].astype(F32), 0.0)).astype(BF16)

    def x_copy(kinds, g, sem, recv):
        return remote(xs.at[kinds, g], xr.at[kinds, g], sent.at[sem], recv, x_peer)

    def back_fill(kind, g):
        chip = earlier(kind, g) + xr[kind, g].astype(F32)
        later = (core == 1) if kind == 1 else (core == 0)
        ours = st[kind, g, core].astype(F32)
        theirs = cr[kind, g].astype(F32)
        ps[kind, g] = jnp.where(later, chip, chip + ours).astype(BF16)
        pr[kind, g, core] = jnp.where(later, chip + theirs, chip).astype(BF16)

    def back_copy(kinds, g, sem, recv):
        return remote(ps.at[kinds, g], pr.at[kinds, g, core], sent.at[sem], recv, core_peer)

    every = pl.ds(0, GROUPS)
    head_start = pl.ds(0, 1)
    rest = pl.ds(1, GROUPS - 1)
    a_core = core_copy(alone, every, 3, a_recv.at[0])
    a_x = [x_copy(alone, part, 4, a_recv.at[1 + n]) for n, part in enumerate((head_start, rest))]
    a_back = [back_copy(alone, part, 5, a_recv.at[3 + n]) for n, part in enumerate((head_start, rest))]
    ay = (0, every, ay_recv, 6)
    a_core.start()

    relay(0)
    relay(1)

    loads[2].wait()
    loads[3].wait()
    wide = 256

    def partial(n, carry):
        at = lanes(n, wide)
        vp[:, at] = dot(x2[0], wv[0, :, at])
        return carry

    lax.fori_loop(0, width // wide, partial, 0)

    a_core.wait_recv()
    pl.semaphore_wait(y_known, 1)
    y_send(*ay)
    relay(2)
    relay(3)

    def turn_own(side):
        def turn(n, carry):
            at = lanes(((head + side) % 2) * 4 + n)
            xt[at, :tokens] = x2[side, :, lanes(2 * n + core)].T
            return carry

        lax.fori_loop(0, 4, turn, 0)

    def turn_theirs(side):
        def turn(n, carry):
            block = ((head + side) % 2) * 4 + n
            xt[lanes(block), tokens:] = xp[block].T
            return carry

        lax.fori_loop(0, 4, turn, 0)

    turn_own(0)
    for copy in swaps:
        copy.wait_recv()
    turn_theirs(0)
    loads[4].wait()
    loads[5].wait()
    y_wait(*ay)
    x_fill(0, head_start)
    a_x[0].start()
    x_fill(0, rest)

    def finish(n):
        for side in range(2):
            for m in (2 * n, 2 * n + 1):
                second[2 * m + side].wait_recv()
        if n == 1:
            a_x[1].start()
        size = 2 * piece

        def values(m, carry):
            at = lanes(m, wide)
            for side in range(2):
                rows = slice(side * mid + n * size, side * mid + (n + 1) * size)
                vv[rows, at] = (vp[rows, at] + dot(x2[1, rows, :], wv[1, :, at])).astype(BF16)
            return carry

        lax.fori_loop(0, width // wide, values, 0)

    finish(0)
    finish(1)
    for n in range(4):
        src = x2.at[1, :, lanes(2 * n + 1 - core)]
        swaps.append(remote(src, xp.at[(1 - head) * 4 + n], sent.at[2], p_recv.at[1, n], core_peer))
        swaps[-1].start()
    a_x[0].wait_recv()
    back_fill(0, head_start)
    a_back[0].start()

    def states(h, carry):
        at = lanes(h)
        g, which, n = h // per_group, lax.rem(h, per_group) // mine, lax.rem(h, mine)
        v = vv[:, at]
        st[1, g, which, n] = dot(kt[h], v).astype(BF16)
        top = dot(sc[h, :mid, :mid], v[:mid])
        bottom = dot(sc[h, mid:, :], v)
        gl[:mid, at] = (gc * top - loss_scale * tv[:mid, at].astype(F32)).astype(BF16)
        gl[mid:, at] = (gc * bottom - loss_scale * tv[mid:, at].astype(F32)).astype(BF16)
        uu[h] = dot(qt[h], gl[:, at])
        return carry

    def with_later(h, carry):
        g, which, n = h // per_group, lax.rem(h, per_group) // mine, lax.rem(h, mine)
        st[2, g, which, n] = (uu[h] + gc * dot(pr[0, g, which, n], st[1, g, which, n])).astype(BF16)
        return carry

    def bases(h, carry):
        at = lanes(h)
        base[:mid, at] = dot(sct[h, :mid, :], gl[:, at])
        base[mid:, at] = dot(sct[h, mid:, mid:], gl[mid:, at])
        return carry

    def over(body, g):
        lax.fori_loop(g * per_group, (g + 1) * per_group, body, 0)

    def gv_copy(g):
        return remote(
            gv.at[g, pl.ds(0, tokens)], gv.at[g, pl.ds(tokens, tokens)], sent.at[18], g_recv.at[g], core_peer
        )

    def grads(g):
        def one(n, carry):
            h = g * per_group + n
            at = lanes(h)
            which, i = n // mine, lax.rem(n, mine)
            prefix = pr[1, g, which, i]
            up_to = (prefix.astype(F32) + st[1, g, which, i].astype(F32)).astype(BF16)
            suffix = (gc * dot(pr[0, g, which, i], up_to) + pr[2, g, which, i].astype(F32)).astype(BF16)
            pair = jnp.concatenate([prefix, suffix], axis=0)
            gv[g, :tokens, lanes(n)] = (attn_scale * (base[:, at] + dot(wqk[h], pair))).astype(BF16)
            return carry

        lax.fori_loop(0, per_group, one, 0)
        copy = gv_copy(g)
        copy.start()

    two = 2 * rows_dev
    part = cols // 2

    def block(g, to):
        return dot(xt[pl.ds(pl.multiple_of(to * two, two), two), :], gv[g])

    def r1_copies(g):
        return (
            remote(s1.at[g, 0], r1.at[g, 0], sent.at[19], r1_recv.at[g, 0], y_up),
            remote(s1.at[g, 1], r1.at[g, 1], sent.at[19], r1_recv.at[g, 1], y_down),
        )

    def r2_copies(g):
        return (
            remote(s2.at[g, 0], r2.at[g, 0], sent.at[20], r2_recv.at[g, 0], y_up),
            remote(s2.at[g, 1], r2.at[g, 1], sent.at[20], r2_recv.at[g, 1], y_down),
        )

    def reduce_one(g):
        gv_copy(g).wait_recv()
        across = block(g, lax.rem(y + 2, 4)).astype(BF16)
        s1[g, 0] = across[:, :part]
        s1[g, 1] = across[:, part:]
        for copy in r1_copies(g):
            copy.start()

    def sides(g):
        up = block(g, lax.rem(y + 1, 4))
        s2[g, 0, :, part:] = up[:, part:].astype(BF16)
        keep[g, 0] = up[:, :part]
        down = block(g, lax.rem(y + 3, 4))
        s2[g, 1, :, :part] = down[:, :part].astype(BF16)
        keep[g, 1] = down[:, part:]

    def reduce_two(g):
        one = r1_copies(g)
        one[0].wait_recv()
        s2[g, 0, :, :part] = (keep[g, 0] + r1[g, 0].astype(F32)).astype(BF16)
        one[1].wait_recv()
        s2[g, 1, :, part:] = (keep[g, 1] + r1[g, 1].astype(F32)).astype(BF16)
        for copy in r2_copies(g):
            copy.start()

    def own_block(g):
        own[g] = block(g, y)

    def rx_copy(g):
        return remote(sx.at[g], rx.at[g], sent.at[21], rx_recv.at[g], x_peer)

    def block_rows(which):
        return pl.ds(pl.multiple_of(which * rows_dev, rows_dev), rows_dev)

    def reduce_x(g):
        for copy in r2_copies(g):
            copy.wait_recv()
        rows = block_rows(1 - xl)
        sx[g] = (own[g, rows, :] + r2[g, 0, rows, :].astype(F32) + r2[g, 1, rows, :].astype(F32)).astype(BF16)
        copy = rx_copy(g)
        copy.start()

    share = rows_dev // 4

    def piece_rows(which):
        return pl.ds(pl.multiple_of(which * share, share), share)

    def rz_copies(g):
        return [
            remote(dz.at[g, piece_rows(z)], rz.at[g, n], sent.at[22], rz_recv.at[g, n], peer)
            for n, (z, peer) in enumerate(zip(z_ids, z_peers))
        ]

    def reduce_z(g):
        rx_copy(g).wait_recv()
        rows = block_rows(xl)
        at = slice(g * cols, (g + 1) * cols)
        total = own[g, rows, :] + r2[g, 0, rows, :].astype(F32) + r2[g, 1, rows, :].astype(F32)
        drift = (av[:, at] - wv[2, :rows_dev, at].astype(F32)) / inner_rate
        dz[g] = (total + rx[g].astype(F32) + drift).astype(BF16)
        for copy in rz_copies(g):
            copy.start()

    def mz_copies(g):
        at = slice(g * cols, (g + 1) * cols)
        return [
            remote(mz.at[g], mixb.at[piece_rows(zk), at], sent.at[23], mz_recv.at[g, n], peer)
            for n, peer in enumerate(z_peers)
        ]

    def mix(g):
        for copy in rz_copies(g):
            copy.wait_recv()
        at = slice(g * cols, (g + 1) * cols)
        total = dz[g, piece_rows(zk), :].astype(F32)
        for n in range(3):
            total += rz[g, n].astype(F32)
        mean = (0.25 * total).astype(BF16)
        mz[g] = mean
        mixb[piece_rows(zk), at] = mean
        for copy in mz_copies(g):
            copy.start()

    def settle(g):
        for copy in mz_copies(g):
            copy.wait_recv()

    loads[6].wait()
    loads[7].wait()

    def scan_core(g):
        return core_copy(both, pl.ds(g, 1), 9, c_recv.at[g])

    def scan_x(g):
        return x_copy(both, pl.ds(g, 1), 10, x_recv.at[g])

    def scan_back(g):
        return back_copy(both, pl.ds(g, 1), 11, b_recv.at[g])

    def y_args(kind, g):
        return (kind, pl.ds(g, 1), y_recv.at[kind - 1, g], 12 + 3 * (kind - 1))

    def state_step(g):
        over(states, g)

    def later_step(g):
        if g < 2:
            a_back[g].wait_recv()
        over(with_later, g)
        scan_core(g).start()

    def later_states():
        a_x[1].wait_recv()
        back_fill(0, rest)
        a_back[1].start()

    def y_step(g):
        scan_core(g).wait_recv()
        for kind in (1, 2):
            y_send(*y_args(kind, g))

    def x_step(g):
        for kind in (1, 2):
            y_wait(*y_args(kind, g))
            x_fill(kind, pl.ds(g, 1))
        scan_x(g).start()

    def back_step(g):
        scan_x(g).wait_recv()
        for kind in (1, 2):
            back_fill(kind, pl.ds(g, 1))
        scan_back(g).start()

    def grad_step(g):
        scan_back(g).wait_recv()
        grads(g)

    def base_step(g):
        over(bases, g)

    def prepare(g):
        turn_own(1)
        for copy in swaps[4:]:
            copy.wait_recv()
        turn_theirs(1)

    def know(g):
        @pl.when(zk == 1)
        def _():
            pl.semaphore_wait(low_known, 1)
            tell(low_known, z_down)

        @pl.when(zk == 2)
        def _():
            pl.semaphore_wait(high_known, 1)
            tell(high_known, z_up)

    def know_all(g):
        @pl.when(zk == 0)
        def _():
            pl.semaphore_wait(low_known, 2)

        @pl.when(zk == 3)
        def _():
            pl.semaphore_wait(high_known, 2)

    steps = {
        "state": state_step,
        "later": later_step,
        "a_rest": lambda g: later_states(),
        "y": y_step,
        "x": x_step,
        "back": back_step,
        "base": base_step,
        "prepare": prepare,
        "know": know,
        "know_all": know_all,
        "grad": grad_step,
        "r1": reduce_one,
        "sides": sides,
        "r2": reduce_two,
        "own": own_block,
        "rx": reduce_x,
        "rz": reduce_z,
        "mix": mix,
        "end": settle,
    }
    for name, g in ORDER:
        steps[name](g)

    out_ref[...] = mixb[...]

    def drain(sem, ref):
        remote(ref, ref, sent.at[sem], sent.at[sem], core_peer).wait_send()

    drain(0, rel)
    drain(1, x2.at[1])
    drain(2, xp)
    drain(3, cr.at[alone])
    drain(4, xs.at[alone])
    drain(5, ps.at[alone])
    for kind in range(3):
        for d in range(3):
            sem = 6 + d if kind == 0 else 12 + 3 * (kind - 1) + d
            pl.when(place(kind) < 3 - d)(functools.partial(drain, sem, yr.at[kind, d]))
    drain(9, cr.at[both])
    drain(10, xs.at[both])
    drain(11, ps.at[both])
    drain(18, gv.at[:, pl.ds(0, tokens)])
    drain(19, s1)
    drain(20, s2)
    drain(21, sx)
    drain(22, rz)
    drain(23, rz)


def mixed_delta(x, q, k, t, w, a, attn_scale, loss_scale):
    tokens, half = x.shape
    width = q.shape[1]
    heads = width // HEAD_DIM
    rows_dev = a.shape[0]
    groups = GROUPS
    per_group = heads // groups
    mine = per_group // 2
    cols = per_group * HEAD_DIM
    two = 2 * rows_dev
    piece = tokens // 2 // CHUNKS
    state = (HEAD_DIM, HEAD_DIM)
    vmem = pltpu.VMEM
    dma = pltpu.SemaphoreType.DMA
    scratch = [
        vmem((2, tokens, half), BF16),
        vmem((8, tokens, HEAD_DIM), BF16),
        vmem((8 * HEAD_DIM, 2 * tokens), BF16),
        vmem((2, CHUNKS, piece, half), BF16),
        vmem((tokens, width), BF16),
        vmem((tokens, width), BF16),
        vmem((tokens, width), BF16),
        vmem((3, half, width), BF16),
        vmem((rows_dev, width), F32),
        vmem((heads, HEAD_DIM, tokens), BF16),
        vmem((heads, HEAD_DIM, tokens), BF16),
        vmem((heads, tokens, tokens), BF16),
        vmem((heads, tokens, tokens), BF16),
        vmem((heads, tokens, 2 * HEAD_DIM), BF16),
        vmem((tokens, width), F32),
        vmem((tokens, width), BF16),
        vmem((tokens, width), BF16),
        vmem((tokens, width), F32),
        vmem((3, groups, 2, mine, *state), BF16),
        vmem((3, groups, mine, *state), BF16),
        vmem((3, groups, mine, *state), BF16),
        vmem((3, 3, groups, mine, *state), BF16),
        vmem((3, groups, mine, *state), BF16),
        vmem((3, groups, mine, *state), BF16),
        vmem((3, groups, mine, *state), BF16),
        vmem((3, groups, 2, mine, *state), BF16),
        vmem((groups, 2 * tokens, cols), BF16),
        vmem((groups, 2, two, cols // 2), F32),
        vmem((groups, 2, two, cols // 2), BF16),
        vmem((groups, 2, two, cols // 2), BF16),
        vmem((groups, 2, two, cols), BF16),
        vmem((groups, 2, two, cols), BF16),
        vmem((groups, two, cols), F32),
        vmem((groups, rows_dev, cols), BF16),
        vmem((groups, rows_dev, cols), BF16),
        vmem((groups, rows_dev, cols), BF16),
        vmem((groups, 3, rows_dev // 4, cols), BF16),
        vmem((groups, rows_dev // 4, cols), BF16),
        vmem((rows_dev, width), BF16),
        vmem((heads, *state), F32),
        dma((8,)),
        dma((24,)),
        dma((4, CHUNKS)),
        dma((2, 4)),
        dma((5,)),
        dma((3,)),
        dma((groups,)),
        dma((2, groups, 3)),
        dma((groups,)),
        dma((groups,)),
        dma((groups,)),
        dma((groups, 2)),
        dma((groups, 2)),
        dma((groups,)),
        dma((groups, 3)),
        dma((groups, 3)),
        pltpu.SemaphoreType.REGULAR,
        pltpu.SemaphoreType.REGULAR,
        pltpu.SemaphoreType.REGULAR,
    ]
    return pl.pallas_call(
        functools.partial(kernel, attn_scale, loss_scale),
        out_shape=jax.ShapeDtypeStruct((rows_dev, width), BF16),
        in_specs=[pl.BlockSpec(memory_space=pl.ANY)] * 6,
        out_specs=pl.BlockSpec(memory_space=pltpu.VMEM),
        scratch_shapes=scratch,
        compiler_params=pltpu.CompilerParams(
            collective_id=0, has_side_effects=True, vmem_limit_bytes=60 * 1024 * 1024
        ),
    )(x, q, k, t, w, a)


def local(inputs, queries, keys, targets, value_weight, anchor, momentum):
    sequence = queries.shape[1] * lax.axis_size("ctx")
    attn_scale = 1.0 / math.sqrt(HEAD_DIM * sequence)
    loss_scale = 1.0 / math.sqrt(sequence)
    mixed = mixed_delta(
        inputs[0], queries[0], keys[0], targets[0], value_weight[0], anchor, attn_scale, loss_scale
    )
    momentum_next = slow_decay * momentum + mixed.astype(F32)
    anchor_next = anchor - outer_rate * inner_rate * momentum_next
    return (anchor_next[None], momentum_next[None])


def solution(mesh):
    placed = (
        P("rep", "ctx", "head"),
        P("rep", "ctx", "head"),
        P("rep", "ctx", "head"),
        P("rep", "ctx", "head"),
        P("rep", None, "head"),
        P("ctx", "head"),
        P("ctx", "head"),
    )
    return jax.shard_map(
        local,
        mesh=mesh,
        in_specs=placed,
        out_specs=(P("rep", "ctx", "head"), P("rep", "ctx", "head")),
        check_vma=False,
    )
```

```python
import functools
import math

import jax
import jax.numpy as jnp
from jax import lax
from jax.experimental import pallas as pl
from jax.experimental.pallas import tpu as pltpu
from jax.sharding import PartitionSpec as P

HEAD_DIM = 128
GROUPS = 4
WIDE = 1
CHUNKS = 4
MESH = pl.DeviceIdType.MESH

ORDER = (
    ("state", 0), ("later", 0), ("a_rest", 0), ("state", 1), ("prepare", 0), ("y", 0), ("state", 3), ("later", 1),
    ("later", 3), ("state", 2), ("base", 1), ("y", 1), ("base", 3), ("base", 2), ("base", 0), ("x", 0),
    ("know", 0), ("y", 3), ("later", 2), ("y", 2), ("x", 1), ("back", 0), ("grad", 0), ("x", 3),
    ("back", 1), ("x", 2), ("r1", 0), ("grad", 1), ("back", 3), ("own", 0), ("sides", 0), ("back", 2),
    ("w0", 1), ("r2", 0), ("grad", 3), ("wo", 1), ("grad", 2), ("r1", 3), ("own", 3), ("sides", 3),
    ("r1", 2), ("rx", 0), ("own", 2), ("sides", 2), ("r2", 3), ("w1", 1), ("r2", 2), ("rz", 0),
    ("rx", 3), ("w2", 1), ("mix", 0), ("rz", 3), ("rx", 2), ("rz", 1), ("end", 0), ("rz", 2),
    ("mix", 3), ("mix", 1), ("mix", 2), ("end", 3), ("end", 1), ("end", 2),
)

inner_rate = 0.05
slow_decay = 0.5
outer_rate = 1.0

F32 = jnp.float32
BF16 = jnp.bfloat16


def dot(a, b):
    return jnp.dot(a, b, preferred_element_type=F32)


def lanes(index, size=HEAD_DIM):
    return pl.ds(pl.multiple_of(index * size, size), size)


def kernel(
    attn_scale,
    loss_scale,
    x_ref,
    q_ref,
    k_ref,
    t_ref,
    w_ref,
    a_ref,
    out_ref,
    x2,
    xp,
    xt,
    rel,
    qv,
    kv,
    tv,
    wv,
    av,
    qt,
    kq,
    sc,
    sct,
    wqk,
    vp,
    vv,
    ww,
    qtt,
    base,
    st,
    cr,
    tt,
    yr,
    xs,
    xr,
    ps,
    pr,
    gv,
    keep,
    s1,
    r1,
    s2,
    r2,
    own,
    sx,
    rx,
    dz,
    rz,
    mz,
    mixb,
    uu,
    wx,
    wo,
    w1,
    w2,
    load_sem,
    sent,
    f_recv,
    h_recv,
    p_recv,
    a_recv,
    ay_recv,
    c_recv,
    y_recv,
    x_recv,
    b_recv,
    g_recv,
    r1_recv,
    r2_recv,
    rx_recv,
    rz_recv,
    mz_recv,
    w_recv,
    y_known,
    low_known,
    high_known,
):
    tokens, width = qv.shape
    half = x2.shape[2]
    heads = width // HEAD_DIM
    per_group = heads // GROUPS
    mine = per_group // 2
    cols = per_group * HEAD_DIM
    rows_dev = av.shape[0]
    gc = loss_scale * attn_scale

    me = lax.axis_index("ctx")
    rep = lax.axis_index("rep")
    head = lax.axis_index("head")
    core = lax.rem(me, 2)
    xl = lax.rem(me // 2, 2)
    y = me // 4
    low = lax.rem(me, 4)
    core_peer = (me + 1 - 2 * core, rep, head)
    x_id = me + 2 - 4 * xl
    x_peer = (x_id, rep, head)
    far_peer = (x_id, rep, 1 - head)
    y_up = (lax.rem(y + 1, 4) * 4 + low, rep, head)
    y_down = (lax.rem(y + 3, 4) * 4 + low, rep, head)
    zk = lax.rem(rep, 4)
    y_far = (lax.rem(y + 2, 4) * 4 + low, rep, head)
    z_up = (me, lax.rem(rep + 1, 8), head)
    z_down = (me, lax.rem(rep + 7, 8), head)
    inner = (zk > 0) & (zk < 3)
    z_peers = [(me, rep - zk + lax.rem(zk + d, 4), head) for d in (1, 2, 3)]
    owners = [(me, rep - zk + z, head) for z in (1, 2)]

    def remote(src, dst, send, recv, peer):
        return pltpu.make_async_remote_copy(
            src_ref=src, dst_ref=dst, send_sem=send, recv_sem=recv, device_id=peer, device_id_type=MESH
        )

    def arrived(sem, ref):
        pltpu.make_async_copy(ref, ref, sem).wait()

    own_rows = pl.ds(pl.multiple_of(head * half, half), half)
    other_rows = pl.ds(pl.multiple_of((1 - head) * half, half), half)
    loads = [
        pltpu.make_async_copy(src, dst, load_sem.at[n])
        for n, (src, dst) in enumerate(
            (
                (q_ref, qv),
                (k_ref, kv),
                (x_ref, x2.at[0]),
                (w_ref.at[own_rows], wv.at[0]),
                (t_ref, tv),
                (w_ref.at[other_rows], wv.at[1]),
                (w_ref.at[pl.ds(pl.multiple_of(me * rows_dev, rows_dev), rows_dev)], wv.at[2, pl.ds(0, rows_dev)]),
                (a_ref, av),
            )
        )
    ]
    for copy in loads:
        copy.start()

    yr[...] = jnp.zeros_like(yr)

    barrier = pltpu.get_barrier_semaphore()
    peers = [core_peer, x_peer, far_peer, y_up, y_down, z_up, z_down]
    for peer in peers:
        pl.semaphore_signal(barrier, inc=1, device_id=peer, device_id_type=MESH)

    pl.semaphore_wait(barrier, len(peers))

    def tell(sem, peer):
        pl.semaphore_signal(sem, inc=1, device_id=peer, device_id_type=MESH)

    piece = tokens // 2 // CHUNKS
    first = []
    for n in range(CHUNKS):
        for side, peer in ((0, x_peer), (1, far_peer)):
            at = side * (tokens // 2) + n * piece
            first.append(
                remote(x_ref.at[pl.ds(at, piece)], rel.at[side, n], sent.at[0], f_recv.at[side, n], peer)
            )
            first[-1].start()
    for n in range(4):
        src = x_ref.at[:, lanes(2 * n + 1 - core)]
        remote(src, xp.at[head * 4 + n], sent.at[0], p_recv.at[0], core_peer).start()

    tell(y_known, y_down)

    @pl.when(inner)
    def _():
        tell(low_known, z_down)
        tell(high_known, z_up)

    def relay(n):
        for side, peer in ((0, far_peer), (1, x_peer)):
            first[2 * n + side].wait_recv()
            at = side * (tokens // 2) + n * piece
            remote(rel.at[side, n], x2.at[1, pl.ds(at, piece)], sent.at[0], h_recv.at[n // 2], peer).start()

    loads[0].wait()
    loads[1].wait()
    mid = tokens // 2

    def scores(h, carry):
        at = lanes(h)
        q = qv[:, at]
        k = kv[:, at]
        q_t = q.T
        k_t = k.T
        qt[h] = q_t
        kq[h, :HEAD_DIM] = k_t
        row = lax.broadcasted_iota(jnp.int32, (mid, mid), 0)
        col = lax.broadcasted_iota(jnp.int32, (mid, mid), 1)
        lower = row >= col
        upper = row <= col
        for n in range(2):
            rows = slice(n * mid, (n + 1) * mid)
            sc[h, rows, rows] = jnp.where(lower, dot(q[rows], k_t[:, rows]), 0.0).astype(BF16)
            sct[h, rows, rows] = jnp.where(upper, dot(k[rows], q_t[:, rows]), 0.0).astype(BF16)
        sc[h, mid:, :mid] = dot(q[mid:], k_t[:, :mid]).astype(BF16)
        sct[h, :mid, mid:] = dot(k[:mid], q_t[:, mid:]).astype(BF16)
        wqk[h, :, HEAD_DIM:] = k
        st[0, h // per_group, lax.rem(h, per_group) // mine, lax.rem(h, mine)] = dot(q_t, q).astype(BF16)
        return carry

    def products(h, carry):
        at = lanes(h)
        q = qv[:, at]
        t = tv[:, at]
        q_t = qt[h]
        wqk[h, :mid, :HEAD_DIM] = (gc * dot(sct[h, :mid, :], q)).astype(BF16)
        wqk[h, mid:, :HEAD_DIM] = (gc * dot(sct[h, mid:, mid:], q[mid:])).astype(BF16)
        kq[h, HEAD_DIM:, :mid] = (gc * dot(q_t, sc[h, :, :mid])).astype(BF16)
        kq[h, HEAD_DIM:, mid:] = (gc * dot(q_t[:, mid:], sc[h, mid:, mid:])).astype(BF16)
        qtt[h] = -loss_scale * dot(q_t, t)
        base[:mid, at] = -loss_scale * dot(sct[h, :mid, :], t)
        base[mid:, at] = -loss_scale * dot(sct[h, mid:, mid:], t[mid:])
        low = dot(sct[h, :mid, mid:], sc[h, mid:, :])
        ww[h, :mid, :mid] = (gc * (low[:, :mid] + dot(sct[h, :mid, :mid], sc[h, :mid, :mid]))).astype(BF16)
        ww[h, :mid, mid:] = (gc * low[:, mid:]).astype(BF16)
        ww[h, mid:, :] = (gc * dot(sct[h, mid:, mid:], sc[h, mid:, :])).astype(BF16)
        return carry

    lax.fori_loop(0, heads, scores, 0)

    both = pl.ds(1, 2)
    alone = pl.ds(0, 1)

    def place(kind):
        return y if kind == 1 else 3 - y

    def core_copy(kinds, g, sem, recv):
        return remote(st.at[kinds, g, 1 - core], cr.at[kinds, g], sent.at[sem], recv, core_peer)

    def y_copies(kind, g, recv):
        ahead, behind = (y_up, y_down) if kind == 1 else (y_down, y_up)
        return [
            remote(tt.at[kind, g], yr.at[kind, d, g], sent.at[3], recv, peer)
            for d, peer in enumerate((ahead, y_far, behind))
        ]

    def y_send(kind, g, recv):
        total = st[kind, g, core].astype(F32) + cr[kind, g].astype(F32)
        tt[kind, g] = total.astype(BF16)
        for d, copy in enumerate(y_copies(kind, g, recv)):
            pl.when(place(kind) < 3 - d)(copy.start)

    def y_wait(kind, g, recv):
        for d in (1, 2, 3):
            pl.when(place(kind) == d)(functools.partial(arrived, recv, yr.at[kind, pl.ds(0, d), g]))

    def earlier(kind, g):
        return yr[kind, 0, g].astype(F32) + yr[kind, 1, g].astype(F32) + yr[kind, 2, g].astype(F32)

    def x_fill(kind, g):
        gives = (xl == 0) if kind == 1 else (xl == 1)
        xs[kind, g] = (earlier(kind, g) + jnp.where(gives, tt[kind, g].astype(F32), 0.0)).astype(BF16)

    def x_copy(kinds, g, sem, recv):
        return remote(xs.at[kinds, g], xr.at[kinds, g], sent.at[sem], recv, x_peer)

    def back_fill(kind, g):
        chip = earlier(kind, g) + xr[kind, g].astype(F32)
        later = (core == 1) if kind == 1 else (core == 0)
        ours = st[kind, g, core].astype(F32)
        theirs = cr[kind, g].astype(F32)
        ps[kind, g] = jnp.where(later, chip, chip + ours).astype(BF16)
        pr[kind, g, core] = jnp.where(later, chip + theirs, chip).astype(BF16)

    def back_copy(kinds, g, sem, recv):
        return remote(ps.at[kinds, g], pr.at[kinds, g, core], sent.at[sem], recv, core_peer)

    every = pl.ds(0, GROUPS)
    head_start = pl.ds(0, 1)
    rest = pl.ds(1, GROUPS - 1)
    a_core = core_copy(alone, every, 2, a_recv.at[0])
    a_x = [x_copy(alone, part, 2, a_recv.at[1 + n]) for n, part in enumerate((head_start, rest))]
    a_back = [back_copy(alone, part, 2, a_recv.at[3 + n]) for n, part in enumerate((head_start, rest))]
    ay = (0, every, ay_recv.at[0])
    a_core.start()

    relay(0)
    a_core.wait_recv()
    pl.semaphore_wait(y_known, 1)
    y_send(*ay)
    relay(1)

    loads[2].wait()
    loads[3].wait()
    wide = 256

    def partial(n, carry):
        at = lanes(n, wide)
        vp[:, at] = dot(x2[0], wv[0, :, at])
        return carry

    lax.fori_loop(0, width // wide, partial, 0)

    loads[4].wait()
    lax.fori_loop(0, 2, products, 0)
    relay(2)
    lax.fori_loop(2, 4, products, 0)
    relay(3)
    y_wait(*ay)
    for copy, which in zip(a_x, (head_start, rest)):
        x_fill(0, which)
        copy.start()
    lax.fori_loop(4, heads, products, 0)

    def turn_own(side):
        def turn(n, carry):
            block = lax.rem(head + side, 2) * 4 + n
            xt[block // 2, lax.rem(block, 2), :, :tokens] = x2[side, :, lanes(2 * n + core)].T
            return carry

        lax.fori_loop(0, 4, turn, 0)

    def turn_theirs(side):
        def turn(n, carry):
            block = lax.rem(head + side, 2) * 4 + n
            xt[block // 2, lax.rem(block, 2), :, tokens:] = xp[block].T
            return carry

        lax.fori_loop(0, 4, turn, 0)

    turn_own(0)
    arrived(p_recv.at[0], xp.at[pl.ds(0, 4)])
    turn_theirs(0)
    loads[5].wait()

    def finish(n):
        size = 2 * piece
        arrived(h_recv.at[n], x2.at[1, pl.ds(0, mid)])
        parts = [slice(side * mid + n * size, side * mid + (n + 1) * size) for side in range(2)]

        def values(m, carry):
            at = lanes(m, wide)
            rows = jnp.concatenate([x2[1, p, :] for p in parts], axis=0)
            got = dot(rows, wv[1, :, at])
            for i, p in enumerate(parts):
                vv[p, at] = (vp[p, at] + got[i * size : (i + 1) * size]).astype(BF16)
            return carry

        lax.fori_loop(0, width // wide, values, 0)

    finish(0)
    a_x[0].wait_recv()
    back_fill(0, head_start)
    a_back[0].start()
    finish(1)
    for n in range(4):
        src = x2.at[1, :, lanes(2 * n + 1 - core)]
        remote(src, xp.at[(1 - head) * 4 + n], sent.at[0], p_recv.at[1], core_peer).start()
    def states(h, carry):
        at = lanes(h)
        g, which, n = h // per_group, lax.rem(h, per_group) // mine, lax.rem(h, mine)
        both_states = dot(kq[h], vv[:, at])
        st[1, g, which, n] = both_states[:HEAD_DIM].astype(BF16)
        uu[h] = both_states[HEAD_DIM:] + qtt[h]
        return carry

    def with_later(h, carry):
        g, which, n = h // per_group, lax.rem(h, per_group) // mine, lax.rem(h, mine)
        st[2, g, which, n] = (uu[h] + gc * dot(pr[0, g, which, n], st[1, g, which, n])).astype(BF16)
        return carry

    def bases(h, carry):
        at = lanes(h)
        base[:, at] += dot(ww[h], vv[:, at])
        return carry

    def over(body, g):
        lax.fori_loop(g * per_group, (g + 1) * per_group, body, 0)

    def gv_copy(g):
        return remote(
            gv.at[g, pl.ds(0, tokens)], gv.at[g, pl.ds(tokens, tokens)], sent.at[1], g_recv.at[g], core_peer
        )

    def grads(g):
        def one(n, carry):
            h = g * per_group + n
            at = lanes(h)
            which, i = n // mine, lax.rem(n, mine)
            prefix = pr[1, g, which, i]
            up_to = (prefix.astype(F32) + st[1, g, which, i].astype(F32)).astype(BF16)
            suffix = (gc * dot(pr[0, g, which, i], up_to) + pr[2, g, which, i].astype(F32)).astype(BF16)
            pair = jnp.concatenate([prefix, suffix], axis=0)
            gv[g, :tokens, lanes(n)] = (attn_scale * (base[:, at] + dot(wqk[h], pair))).astype(BF16)
            return carry

        lax.fori_loop(0, per_group, one, 0)
        copy = gv_copy(g)
        copy.start()

    two = 2 * rows_dev
    part = cols // 2

    def block(g, to):
        return dot(xt[to].reshape(two, 2 * tokens), gv[g])

    def strip(g, to):
        return dot(xt[:, to].reshape(4 * rows_dev, 2 * tokens), gv[g]).reshape(4, rows_dev, cols)

    def r1_copies(g):
        return (
            remote(s1.at[g, 0], r1.at[g, 0], sent.at[2], r1_recv.at[g], y_up),
            remote(s1.at[g, 1], r1.at[g, 1], sent.at[2], r1_recv.at[g], y_down),
        )

    def r2_copies(g):
        return (
            remote(s2.at[g, 0], r2.at[g, 0], sent.at[2], r2_recv.at[g], y_up),
            remote(s2.at[g, 1], r2.at[g, 1], sent.at[2], r2_recv.at[g], y_down),
        )

    def reduce_one(g):
        gv_copy(g).wait_recv()
        across = block(g, lax.rem(y + 2, 4)).astype(BF16)
        s1[g, 0] = across[:, :part]
        s1[g, 1] = across[:, part:]
        for copy in r1_copies(g):
            copy.start()

    def sides(g):
        up = block(g, lax.rem(y + 1, 4))
        s2[g, 0, :, part:] = up[:, part:].astype(BF16)
        keep[g, 0] = up[:, :part]
        down = block(g, lax.rem(y + 3, 4))
        s2[g, 1, :, :part] = down[:, :part].astype(BF16)
        keep[g, 1] = down[:, part:]

    def reduce_two(g):
        arrived(r1_recv.at[g], r1.at[g])
        s2[g, 0, :, :part] = (keep[g, 0] + r1[g, 0].astype(F32)).astype(BF16)
        s2[g, 1, :, part:] = (keep[g, 1] + r1[g, 1].astype(F32)).astype(BF16)
        for copy in r2_copies(g):
            copy.start()

    def own_block(g):
        own[g] = block(g, y)

    def rx_copy(g):
        return remote(sx.at[g], rx.at[g], sent.at[2], rx_recv.at[g], x_peer)

    def block_rows(which):
        return pl.ds(pl.multiple_of(which * rows_dev, rows_dev), rows_dev)

    def reduce_x(g):
        arrived(r2_recv.at[g], r2.at[g])
        rows = block_rows(1 - xl)
        sx[g] = (own[g, rows, :] + r2[g, 0, rows, :].astype(F32) + r2[g, 1, rows, :].astype(F32)).astype(BF16)
        copy = rx_copy(g)
        copy.start()

    def wx_copy():
        return remote(wx.at[0], wx.at[1], sent.at[1], w_recv.at[0], x_peer)

    def wide_out(g):
        arrived(g_recv.at[g], gv.at[g, pl.ds(0, tokens)])
        wx[0] = strip(g, 1 - xl).astype(BF16)
        wx_copy().start()

    def wide_own(g):
        wo[...] = strip(g, xl)

    def wide_block(at):
        return wo[at] + wx[1, at].astype(F32)

    def w1_copies():
        return [remote(w1.at[0, n], w1.at[1, n], sent.at[2], w_recv.at[1], p) for n, p in enumerate((y_up, y_down))]

    def w2_copies():
        return [remote(w2.at[0, n], w2.at[1, n], sent.at[2], w_recv.at[2], p) for n, p in enumerate((y_up, y_down))]

    def wide_one(g):
        wx_copy().wait_recv()
        across = wide_block(lax.rem(y + 2, 4)).astype(BF16)
        w1[0, 0] = across[:, :part]
        w1[0, 1] = across[:, part:]
        for copy in w1_copies():
            copy.start()

    def wide_two(g):
        up = wide_block(lax.rem(y + 1, 4))
        down = wide_block(lax.rem(y + 3, 4))
        arrived(w_recv.at[1], w1.at[1])
        w2[0, 0, :, :part] = (up[:, :part] + w1[1, 0].astype(F32)).astype(BF16)
        w2[0, 0, :, part:] = up[:, part:].astype(BF16)
        w2[0, 1, :, :part] = down[:, :part].astype(BF16)
        w2[0, 1, :, part:] = (down[:, part:] + w1[1, 1].astype(F32)).astype(BF16)
        for copy in w2_copies():
            copy.start()

    share = rows_dev // 2
    own_share = pl.ds(pl.multiple_of(jnp.where(zk == 2, share, 0), share), share)

    def rz_copies(g):
        return [
            remote(
                dz.at[g, pl.ds(n * share, share)],
                rz.at[g, zk - jnp.where(zk > n + 1, 1, 0)],
                sent.at[4],
                rz_recv.at[g],
                owners[n],
            )
            for n in range(2)
        ]

    def reduce_z(g):
        at = slice(g * cols, (g + 1) * cols)
        if g == WIDE:
            arrived(w_recv.at[2], w2.at[1])
            total = wide_block(y) + w2[1, 0].astype(F32) + w2[1, 1].astype(F32)
        else:
            rx_copy(g).wait_recv()
            rows = block_rows(xl)
            total = own[g, rows, :] + r2[g, 0, rows, :].astype(F32) + r2[g, 1, rows, :].astype(F32)
            total += rx[g].astype(F32)
        drift = (av[:, at] - wv[2, :rows_dev, at].astype(F32)) / inner_rate
        dz[g] = (total + drift).astype(BF16)
        for n, copy in enumerate(rz_copies(g)):
            pl.when(zk != n + 1)(copy.start)

    def mix(g):
        @pl.when(inner)
        def _():
            arrived(rz_recv.at[g], rz.at[g])
            at = slice(g * cols, (g + 1) * cols)
            total = dz[g, own_share, :].astype(F32)
            for n in range(3):
                total += rz[g, n].astype(F32)
            mean = (0.25 * total).astype(BF16)
            mz[g] = mean
            mixb[own_share, at] = mean
            for peer in z_peers:
                remote(mz.at[g], mixb.at[own_share, at], sent.at[4], mz_recv.at[g], peer).start()

    def settle(g):
        pl.when(inner)(functools.partial(arrived, mz_recv.at[g], mz.at[g]))
        pl.when(~inner)(functools.partial(arrived, mz_recv.at[g], dz.at[g]))

    loads[6].wait()
    loads[7].wait()

    def scan_core(g):
        return core_copy(both, pl.ds(g, 1), 1, c_recv.at[g])

    def scan_x(g):
        return x_copy(both, pl.ds(g, 1), 1, x_recv.at[g])

    def scan_back(g):
        return back_copy(both, pl.ds(g, 1), 1, b_recv.at[g])

    def y_args(kind, g):
        return (kind, pl.ds(g, 1), y_recv.at[kind - 1, g])

    def state_step(g):
        over(states, g)

    def later_step(g):
        if g < 2:
            a_back[g].wait_recv()
        over(with_later, g)
        scan_core(g).start()

    def later_states():
        a_x[1].wait_recv()
        back_fill(0, rest)
        a_back[1].start()

    def y_step(g):
        scan_core(g).wait_recv()
        for kind in (1, 2):
            y_send(*y_args(kind, g))

    def x_step(g):
        for kind in (1, 2):
            y_wait(*y_args(kind, g))
            x_fill(kind, pl.ds(g, 1))
        scan_x(g).start()

    def back_step(g):
        scan_x(g).wait_recv()
        for kind in (1, 2):
            back_fill(kind, pl.ds(g, 1))
        scan_back(g).start()

    def grad_step(g):
        scan_back(g).wait_recv()
        grads(g)

    def base_step(g):
        over(bases, g)

    def prepare(g):
        turn_own(1)
        arrived(p_recv.at[1], xp.at[pl.ds(0, 4)])
        turn_theirs(1)

    def know(g):
        @pl.when(zk < 2)
        def _():
            pl.semaphore_wait(low_known, 1)

        @pl.when(zk >= 2)
        def _():
            pl.semaphore_wait(high_known, 1)

    steps = {
        "state": state_step,
        "later": later_step,
        "a_rest": lambda g: later_states(),
        "y": y_step,
        "x": x_step,
        "back": back_step,
        "base": base_step,
        "prepare": prepare,
        "know": know,
        "grad": grad_step,
        "w0": wide_out,
        "wo": wide_own,
        "w1": wide_one,
        "w2": wide_two,
        "r1": reduce_one,
        "sides": sides,
        "r2": reduce_two,
        "own": own_block,
        "rx": reduce_x,
        "rz": reduce_z,
        "mix": mix,
        "end": settle,
    }
    for name, g in ORDER:
        steps[name](g)

    out_ref[...] = mixb[...]

    def drain(sem, ref):
        remote(ref, ref, sent.at[sem], sent.at[sem], core_peer).wait_send()

    drain(0, wv.at[pl.ds(0, 3), pl.ds(0, tokens)])
    drain(1, x2)
    drain(2, vp.at[pl.ds(0, 15 * tokens // 16)])
    unit = tokens // 8
    for n in range(4):
        pl.when(y == n)(functools.partial(drain, 3, vv.at[pl.ds(0, (3 + n) * unit)]))
    pl.when(inner)(functools.partial(drain, 4, vv.at[pl.ds(0, tokens // 2)]))
    pl.when(~inner)(functools.partial(drain, 4, dz))


def mixed_delta(x, q, k, t, w, a, attn_scale, loss_scale):
    tokens, half = x.shape
    width = q.shape[1]
    heads = width // HEAD_DIM
    rows_dev = a.shape[0]
    groups = GROUPS
    per_group = heads // groups
    mine = per_group // 2
    cols = per_group * HEAD_DIM
    two = 2 * rows_dev
    piece = tokens // 2 // CHUNKS
    state = (HEAD_DIM, HEAD_DIM)
    vmem = pltpu.VMEM
    dma = pltpu.SemaphoreType.DMA
    scratch = [
        vmem((2, tokens, half), BF16),
        vmem((8, tokens, HEAD_DIM), BF16),
        vmem((4, 2, rows_dev, 2 * tokens), BF16),
        vmem((2, CHUNKS, piece, half), BF16),
        vmem((tokens, width), BF16),
        vmem((tokens, width), BF16),
        vmem((tokens, width), BF16),
        vmem((3, half, width), BF16),
        vmem((rows_dev, width), F32),
        vmem((heads, HEAD_DIM, tokens), BF16),
        vmem((heads, 2 * HEAD_DIM, tokens), BF16),
        vmem((heads, tokens, tokens), BF16),
        vmem((heads, tokens, tokens), BF16),
        vmem((heads, tokens, 2 * HEAD_DIM), BF16),
        vmem((tokens, width), F32),
        vmem((tokens, width), BF16),
        vmem((heads, tokens, tokens), BF16),
        vmem((heads, *state), F32),
        vmem((tokens, width), F32),
        vmem((3, groups, 2, mine, *state), BF16),
        vmem((3, groups, mine, *state), BF16),
        vmem((3, groups, mine, *state), BF16),
        vmem((3, 3, groups, mine, *state), BF16),
        vmem((3, groups, mine, *state), BF16),
        vmem((3, groups, mine, *state), BF16),
        vmem((3, groups, mine, *state), BF16),
        vmem((3, groups, 2, mine, *state), BF16),
        vmem((groups, 2 * tokens, cols), BF16),
        vmem((groups, 2, two, cols // 2), F32),
        vmem((groups, 2, two, cols // 2), BF16),
        vmem((groups, 2, two, cols // 2), BF16),
        vmem((groups, 2, two, cols), BF16),
        vmem((groups, 2, two, cols), BF16),
        vmem((groups, two, cols), F32),
        vmem((groups, rows_dev, cols), BF16),
        vmem((groups, rows_dev, cols), BF16),
        vmem((groups, rows_dev, cols), BF16),
        vmem((groups, 3, rows_dev // 2, cols), BF16),
        vmem((groups, rows_dev // 2, cols), BF16),
        vmem((rows_dev, width), BF16),
        vmem((heads, *state), F32),
        vmem((2, 4, rows_dev, cols), BF16),
        vmem((4, rows_dev, cols), F32),
        vmem((2, 2, rows_dev, cols // 2), BF16),
        vmem((2, 2, rows_dev, cols), BF16),
        dma((8,)),
        dma((5,)),
        dma((2, CHUNKS)),
        dma((2,)),
        dma((2,)),
        dma((5,)),
        dma((1,)),
        dma((groups,)),
        dma((2, groups)),
        dma((groups,)),
        dma((groups,)),
        dma((groups,)),
        dma((groups,)),
        dma((groups,)),
        dma((groups,)),
        dma((groups,)),
        dma((groups,)),
        dma((3,)),
        pltpu.SemaphoreType.REGULAR,
        pltpu.SemaphoreType.REGULAR,
        pltpu.SemaphoreType.REGULAR,
    ]
    return pl.pallas_call(
        functools.partial(kernel, attn_scale, loss_scale),
        out_shape=pltpu.VMEM((rows_dev, width), BF16),
        in_specs=[pl.BlockSpec(memory_space=pl.ANY)] * 6,
        out_specs=pl.BlockSpec(memory_space=pltpu.VMEM),
        scratch_shapes=scratch,
        compiler_params=pltpu.CompilerParams(
            collective_id=0, has_side_effects=True, vmem_limit_bytes=60 * 1024 * 1024
        ),
    )(x, q, k, t, w, a)


def local(inputs, queries, keys, targets, value_weight, anchor, momentum):
    sequence = queries.shape[1] * lax.axis_size("ctx")
    attn_scale = 1.0 / math.sqrt(HEAD_DIM * sequence)
    loss_scale = 1.0 / math.sqrt(sequence)
    mixed = mixed_delta(
        inputs[0], queries[0], keys[0], targets[0], value_weight[0], anchor, attn_scale, loss_scale
    )
    momentum_next = slow_decay * momentum + mixed.astype(F32)
    anchor_next = anchor - outer_rate * inner_rate * momentum_next
    return (anchor_next[None], momentum_next[None])


def solution(mesh):
    placed = (
        P("rep", "ctx", "head"),
        P("rep", "ctx", "head"),
        P("rep", "ctx", "head"),
        P("rep", "ctx", "head"),
        P("rep", None, "head"),
        P("ctx", "head"),
        P("ctx", "head"),
    )
    return jax.shard_map(
        local,
        mesh=mesh,
        in_specs=placed,
        out_specs=(P("rep", "ctx", "head"), P("rep", "ctx", "head")),
        check_vma=False,
    )
```

```python
import functools
import math

import jax
import jax.numpy as jnp
from jax import lax
from jax.experimental import pallas as pl
from jax.experimental.pallas import tpu as pltpu
from jax.sharding import PartitionSpec as P

HEAD_DIM = 128
GROUPS = 4
WIDE = 2
CHUNKS = 4
MESH = pl.DeviceIdType.MESH

ORDER = (
    ("state", 0), ("later", 0), ("know", 0), ("a_rest", 0), ("state", 2), ("prepare", 0), ("y", 0), ("later", 2),
    ("state", 1), ("later", 1), ("state", 3), ("later", 3), ("y", 2), ("base", 0), ("y", 1), ("base", 3),
    ("y", 3), ("base", 1), ("x", 0), ("base", 2), ("x", 2), ("back", 0), ("x", 1), ("grad", 0),
    ("back", 2), ("x", 3), ("back", 1), ("r1", 0), ("grad", 2), ("own", 0), ("sides", 0), ("back", 3),
    ("grad", 1), ("r2", 0), ("w0", 2), ("grad", 3), ("r1", 1), ("own", 1), ("sides", 1), ("wo", 2),
    ("r1", 3), ("own", 3), ("sides", 3), ("rx", 0), ("r2", 1), ("w1", 2), ("r2", 3), ("rz", 0),
    ("rx", 1), ("w2", 2), ("mix", 0), ("rx", 3), ("rz", 1), ("rz", 2), ("rz", 3), ("end", 0),
    ("mix", 1), ("mix", 2), ("mix", 3), ("end", 1), ("end", 2), ("end", 3),
)

inner_rate = 0.05
slow_decay = 0.5
outer_rate = 1.0

F32 = jnp.float32
BF16 = jnp.bfloat16


def dot(a, b):
    return jnp.dot(a, b, preferred_element_type=F32)


def lanes(index, size=HEAD_DIM):
    return pl.ds(pl.multiple_of(index * size, size), size)


def kernel(
    attn_scale,
    loss_scale,
    x_ref,
    q_ref,
    k_ref,
    t_ref,
    w_ref,
    a_ref,
    out_ref,
    x2,
    xp,
    xt,
    rel,
    qv,
    kv,
    tv,
    wv,
    av,
    qt,
    kq,
    sc,
    sct,
    wqk,
    vp,
    vv,
    ww,
    qtt,
    base,
    st,
    cr,
    tt,
    yr,
    xs,
    xr,
    ps,
    pr,
    gv,
    keep,
    s1,
    r1,
    s2,
    r2,
    own,
    sx,
    rx,
    dz,
    rz,
    mz,
    mixb,
    uu,
    wx,
    wo,
    w1,
    w2,
    load_sem,
    sent,
    f_recv,
    h_recv,
    p_recv,
    a_recv,
    ay_recv,
    c_recv,
    y_recv,
    x_recv,
    b_recv,
    g_recv,
    r1_recv,
    r2_recv,
    rx_recv,
    rz_recv,
    mz_recv,
    w_recv,
    y_known,
    low_known,
    high_known,
):
    tokens, width = qv.shape
    half = x2.shape[2]
    heads = width // HEAD_DIM
    per_group = heads // GROUPS
    mine = per_group // 2
    cols = per_group * HEAD_DIM
    rows_dev = av.shape[0]
    gc = loss_scale * attn_scale

    me = lax.axis_index("ctx")
    rep = lax.axis_index("rep")
    head = lax.axis_index("head")
    core = lax.rem(me, 2)
    xl = lax.rem(me // 2, 2)
    y = me // 4
    low = lax.rem(me, 4)
    core_peer = (me + 1 - 2 * core, rep, head)
    x_id = me + 2 - 4 * xl
    x_peer = (x_id, rep, head)
    far_peer = (x_id, rep, 1 - head)
    y_up = (lax.rem(y + 1, 4) * 4 + low, rep, head)
    y_down = (lax.rem(y + 3, 4) * 4 + low, rep, head)
    zk = lax.rem(rep, 4)
    y_far = (lax.rem(y + 2, 4) * 4 + low, rep, head)
    z_up = (me, lax.rem(rep + 1, 8), head)
    z_down = (me, lax.rem(rep + 7, 8), head)
    inner = (zk > 0) & (zk < 3)
    z_peers = [(me, rep - zk + lax.rem(zk + d, 4), head) for d in (1, 2, 3)]
    owners = [(me, rep - zk + z, head) for z in (1, 2)]

    def remote(src, dst, send, recv, peer):
        return pltpu.make_async_remote_copy(
            src_ref=src, dst_ref=dst, send_sem=send, recv_sem=recv, device_id=peer, device_id_type=MESH
        )

    def arrived(sem, ref):
        pltpu.make_async_copy(ref, ref, sem).wait()

    own_rows = pl.ds(pl.multiple_of(head * half, half), half)
    other_rows = pl.ds(pl.multiple_of((1 - head) * half, half), half)
    loads = [
        pltpu.make_async_copy(src, dst, load_sem.at[n])
        for n, (src, dst) in enumerate(
            (
                (q_ref, qv),
                (k_ref, kv),
                (x_ref, x2.at[0]),
                (w_ref.at[own_rows], wv.at[0]),
                (t_ref, tv),
                (w_ref.at[other_rows], wv.at[1]),
                (w_ref.at[pl.ds(pl.multiple_of(me * rows_dev, rows_dev), rows_dev)], wv.at[2, pl.ds(0, rows_dev)]),
                (a_ref, av),
            )
        )
    ]
    for copy in loads:
        copy.start()

    yr[...] = jnp.zeros_like(yr)

    barrier = pltpu.get_barrier_semaphore()
    peers = [core_peer, x_peer, far_peer, y_up, y_down, z_up, z_down]
    for peer in peers:
        pl.semaphore_signal(barrier, inc=1, device_id=peer, device_id_type=MESH)

    pl.semaphore_wait(barrier, len(peers))

    def tell(sem, peer):
        pl.semaphore_signal(sem, inc=1, device_id=peer, device_id_type=MESH)

    piece = tokens // 2 // CHUNKS
    first = []
    for n in range(CHUNKS):
        for side, peer in ((0, x_peer), (1, far_peer)):
            at = side * (tokens // 2) + n * piece
            first.append(
                remote(x_ref.at[pl.ds(at, piece)], rel.at[side, n], sent.at[0], f_recv.at[side, n], peer)
            )
            first[-1].start()
    for n in range(4):
        src = x_ref.at[:, lanes(2 * n + 1 - core)]
        remote(src, xp.at[head * 4 + n], sent.at[0], p_recv.at[0], core_peer).start()

    tell(y_known, y_down)

    @pl.when(inner)
    def _():
        tell(low_known, z_down)
        tell(high_known, z_up)

    def relay(n):
        for side, peer in ((0, far_peer), (1, x_peer)):
            first[2 * n + side].wait_recv()
            at = side * (tokens // 2) + n * piece
            remote(rel.at[side, n], x2.at[1, pl.ds(at, piece)], sent.at[0], h_recv.at[n // 2], peer).start()

    loads[0].wait()
    loads[1].wait()
    mid = tokens // 2

    def scores(h, carry):
        at = lanes(h)
        q = qv[:, at]
        k = kv[:, at]
        q_t = q.T
        k_t = k.T
        qt[h] = q_t
        kq[h, :HEAD_DIM] = k_t
        row = lax.broadcasted_iota(jnp.int32, (mid, mid), 0)
        col = lax.broadcasted_iota(jnp.int32, (mid, mid), 1)
        lower = row >= col
        upper = row <= col
        for n in range(2):
            rows = slice(n * mid, (n + 1) * mid)
            sc[h, rows, rows] = jnp.where(lower, dot(q[rows], k_t[:, rows]), 0.0).astype(BF16)
            sct[h, rows, rows] = jnp.where(upper, dot(k[rows], q_t[:, rows]), 0.0).astype(BF16)
        sc[h, mid:, :mid] = dot(q[mid:], k_t[:, :mid]).astype(BF16)
        sct[h, :mid, mid:] = dot(k[:mid], q_t[:, mid:]).astype(BF16)
        wqk[h, :, HEAD_DIM:] = k
        st[0, h // per_group, lax.rem(h, per_group) // mine, lax.rem(h, mine)] = dot(q_t, q).astype(BF16)
        return carry

    def products(h, carry):
        at = lanes(h)
        q = qv[:, at]
        t = tv[:, at]
        q_t = qt[h]
        wqk[h, :mid, :HEAD_DIM] = (gc * dot(sct[h, :mid, :], q)).astype(BF16)
        wqk[h, mid:, :HEAD_DIM] = (gc * dot(sct[h, mid:, mid:], q[mid:])).astype(BF16)
        kq[h, HEAD_DIM:, :mid] = (gc * dot(q_t, sc[h, :, :mid])).astype(BF16)
        kq[h, HEAD_DIM:, mid:] = (gc * dot(q_t[:, mid:], sc[h, mid:, mid:])).astype(BF16)
        qtt[h] = -loss_scale * dot(q_t, t)
        base[:mid, at] = -loss_scale * dot(sct[h, :mid, :], t)
        base[mid:, at] = -loss_scale * dot(sct[h, mid:, mid:], t[mid:])
        low = dot(sct[h, :mid, mid:], sc[h, mid:, :])
        ww[h, :mid, :mid] = (gc * (low[:, :mid] + dot(sct[h, :mid, :mid], sc[h, :mid, :mid]))).astype(BF16)
        ww[h, :mid, mid:] = (gc * low[:, mid:]).astype(BF16)
        ww[h, mid:, :] = (gc * dot(sct[h, mid:, mid:], sc[h, mid:, :])).astype(BF16)
        return carry

    lax.fori_loop(0, heads, scores, 0)

    both = pl.ds(1, 2)
    alone = pl.ds(0, 1)

    def place(kind):
        return y if kind == 1 else 3 - y

    def core_copy(kinds, g, sem, recv):
        return remote(st.at[kinds, g, 1 - core], cr.at[kinds, g], sent.at[sem], recv, core_peer)

    def y_copies(kind, g, recv):
        ahead, behind = (y_up, y_down) if kind == 1 else (y_down, y_up)
        return [
            remote(tt.at[kind, g], yr.at[kind, d, g], sent.at[3], recv, peer)
            for d, peer in enumerate((ahead, y_far, behind))
        ]

    def y_send(kind, g, recv):
        total = st[kind, g, core].astype(F32) + cr[kind, g].astype(F32)
        tt[kind, g] = total.astype(BF16)
        for d, copy in enumerate(y_copies(kind, g, recv)):
            pl.when(place(kind) < 3 - d)(copy.start)

    def y_wait(kind, g, recv):
        for d in (1, 2, 3):
            pl.when(place(kind) == d)(functools.partial(arrived, recv, yr.at[kind, pl.ds(0, d), g]))

    def earlier(kind, g):
        return yr[kind, 0, g].astype(F32) + yr[kind, 1, g].astype(F32) + yr[kind, 2, g].astype(F32)

    def x_fill(kind, g):
        gives = (xl == 0) if kind == 1 else (xl == 1)
        xs[kind, g] = (earlier(kind, g) + jnp.where(gives, tt[kind, g].astype(F32), 0.0)).astype(BF16)

    def x_copy(kinds, g, sem, recv):
        return remote(xs.at[kinds, g], xr.at[kinds, g], sent.at[sem], recv, x_peer)

    def back_fill(kind, g):
        chip = earlier(kind, g) + xr[kind, g].astype(F32)
        later = (core == 1) if kind == 1 else (core == 0)
        ours = st[kind, g, core].astype(F32)
        theirs = cr[kind, g].astype(F32)
        ps[kind, g] = jnp.where(later, chip, chip + ours).astype(BF16)
        pr[kind, g, core] = jnp.where(later, chip + theirs, chip).astype(BF16)

    def back_copy(kinds, g, sem, recv):
        return remote(ps.at[kinds, g], pr.at[kinds, g, core], sent.at[sem], recv, core_peer)

    every = pl.ds(0, GROUPS)
    head_start = pl.ds(0, 1)
    rest = pl.ds(1, GROUPS - 1)
    a_core = core_copy(alone, every, 2, a_recv.at[0])
    a_x = [x_copy(alone, part, 2, a_recv.at[1 + n]) for n, part in enumerate((head_start, rest))]
    a_back = [back_copy(alone, part, 2, a_recv.at[3 + n]) for n, part in enumerate((head_start, rest))]
    ay = (0, every, ay_recv.at[0])
    a_core.start()

    relay(0)
    a_core.wait_recv()
    pl.semaphore_wait(y_known, 1)
    y_send(*ay)
    relay(1)

    loads[2].wait()
    loads[3].wait()
    wide = 256

    def partial(n, carry):
        at = lanes(n, wide)
        vp[:, at] = dot(x2[0], wv[0, :, at])
        return carry

    lax.fori_loop(0, width // wide, partial, 0)

    loads[4].wait()
    lax.fori_loop(0, 2, products, 0)
    relay(2)
    lax.fori_loop(2, 4, products, 0)
    relay(3)
    y_wait(*ay)
    for copy, which in zip(a_x, (head_start, rest)):
        x_fill(0, which)
        copy.start()
    lax.fori_loop(4, heads, products, 0)

    def turn_own(side):
        def turn(n, carry):
            block = lax.rem(head + side, 2) * 4 + n
            xt[block // 2, lax.rem(block, 2), :, :tokens] = x2[side, :, lanes(2 * n + core)].T
            return carry

        lax.fori_loop(0, 4, turn, 0)

    def turn_theirs(side):
        def turn(n, carry):
            block = lax.rem(head + side, 2) * 4 + n
            xt[block // 2, lax.rem(block, 2), :, tokens:] = xp[block].T
            return carry

        lax.fori_loop(0, 4, turn, 0)

    turn_own(0)
    arrived(p_recv.at[0], xp.at[pl.ds(0, 4)])
    turn_theirs(0)
    loads[5].wait()

    def finish(n):
        size = 2 * piece
        arrived(h_recv.at[n], x2.at[1, pl.ds(0, mid)])
        parts = [slice(side * mid + n * size, side * mid + (n + 1) * size) for side in range(2)]

        def values(m, carry):
            at = lanes(m, wide)
            rows = jnp.concatenate([x2[1, p, :] for p in parts], axis=0)
            got = dot(rows, wv[1, :, at])
            for i, p in enumerate(parts):
                vv[p, at] = (vp[p, at] + got[i * size : (i + 1) * size]).astype(BF16)
            return carry

        tiles = width // wide
        lax.fori_loop(0, tiles // 2, values, 0)
        if n == 1:
            a_x[0].wait_recv()
            back_fill(0, head_start)
            a_back[0].start()
        lax.fori_loop(tiles // 2, tiles, values, 0)

    finish(0)
    finish(1)
    for n in range(4):
        src = x2.at[1, :, lanes(2 * n + 1 - core)]
        remote(src, xp.at[(1 - head) * 4 + n], sent.at[0], p_recv.at[1], core_peer).start()
    def states(h, carry):
        at = lanes(h)
        g, which, n = h // per_group, lax.rem(h, per_group) // mine, lax.rem(h, mine)
        both_states = dot(kq[h], vv[:, at])
        st[1, g, which, n] = both_states[:HEAD_DIM].astype(BF16)
        uu[h] = both_states[HEAD_DIM:] + qtt[h]
        return carry

    def with_later(h, carry):
        g, which, n = h // per_group, lax.rem(h, per_group) // mine, lax.rem(h, mine)
        st[2, g, which, n] = (uu[h] + gc * dot(pr[0, g, which, n], st[1, g, which, n])).astype(BF16)
        return carry

    def bases(h, carry):
        at = lanes(h)
        base[:, at] += dot(ww[h], vv[:, at])
        return carry

    def over(body, g):
        lax.fori_loop(g * per_group, (g + 1) * per_group, body, 0)

    def gv_copy(g):
        return remote(
            gv.at[g, pl.ds(0, tokens)], gv.at[g, pl.ds(tokens, tokens)], sent.at[1], g_recv.at[g], core_peer
        )

    def grads(g):
        def one(n, carry):
            h = g * per_group + n
            at = lanes(h)
            which, i = n // mine, lax.rem(n, mine)
            prefix = pr[1, g, which, i]
            up_to = (prefix.astype(F32) + st[1, g, which, i].astype(F32)).astype(BF16)
            suffix = (gc * dot(pr[0, g, which, i], up_to) + pr[2, g, which, i].astype(F32)).astype(BF16)
            pair = jnp.concatenate([prefix, suffix], axis=0)
            gv[g, :tokens, lanes(n)] = (attn_scale * (base[:, at] + dot(wqk[h], pair))).astype(BF16)
            return carry

        lax.fori_loop(0, per_group, one, 0)
        copy = gv_copy(g)
        copy.start()

    two = 2 * rows_dev
    part = cols // 2

    def block(g, to):
        return dot(xt[to].reshape(two, 2 * tokens), gv[g])

    def strip(g, to):
        return dot(xt[:, to].reshape(4 * rows_dev, 2 * tokens), gv[g]).reshape(4, rows_dev, cols)

    def r1_copies(g):
        return (
            remote(s1.at[g, 0], r1.at[g, 0], sent.at[2], r1_recv.at[g], y_up),
            remote(s1.at[g, 1], r1.at[g, 1], sent.at[2], r1_recv.at[g], y_down),
        )

    def r2_copies(g):
        return (
            remote(s2.at[g, 0], r2.at[g, 0], sent.at[2], r2_recv.at[g], y_up),
            remote(s2.at[g, 1], r2.at[g, 1], sent.at[2], r2_recv.at[g], y_down),
        )

    def reduce_one(g):
        gv_copy(g).wait_recv()
        across = block(g, lax.rem(y + 2, 4)).astype(BF16)
        s1[g, 0] = across[:, :part]
        s1[g, 1] = across[:, part:]
        for copy in r1_copies(g):
            copy.start()

    def sides(g):
        up = block(g, lax.rem(y + 1, 4))
        s2[g, 0, :, part:] = up[:, part:].astype(BF16)
        keep[g, 0] = up[:, :part]
        down = block(g, lax.rem(y + 3, 4))
        s2[g, 1, :, :part] = down[:, :part].astype(BF16)
        keep[g, 1] = down[:, part:]

    def reduce_two(g):
        arrived(r1_recv.at[g], r1.at[g])
        s2[g, 0, :, :part] = (keep[g, 0] + r1[g, 0].astype(F32)).astype(BF16)
        s2[g, 1, :, part:] = (keep[g, 1] + r1[g, 1].astype(F32)).astype(BF16)
        for copy in r2_copies(g):
            copy.start()

    def own_block(g):
        own[g] = block(g, y)

    def rx_copy(g):
        return remote(sx.at[g], rx.at[g], sent.at[2], rx_recv.at[g], x_peer)

    def block_rows(which):
        return pl.ds(pl.multiple_of(which * rows_dev, rows_dev), rows_dev)

    def reduce_x(g):
        arrived(r2_recv.at[g], r2.at[g])
        rows = block_rows(1 - xl)
        sx[g] = (own[g, rows, :] + r2[g, 0, rows, :].astype(F32) + r2[g, 1, rows, :].astype(F32)).astype(BF16)
        copy = rx_copy(g)
        copy.start()

    def wx_copy():
        return remote(wx.at[0], wx.at[1], sent.at[1], w_recv.at[0], x_peer)

    def wide_out(g):
        arrived(g_recv.at[g], gv.at[g, pl.ds(0, tokens)])
        wx[0] = strip(g, 1 - xl).astype(BF16)
        wx_copy().start()

    def wide_own(g):
        wo[...] = strip(g, xl)

    def wide_block(at):
        return wo[at] + wx[1, at].astype(F32)

    def w1_copies():
        return [remote(w1.at[0, n], w1.at[1, n], sent.at[2], w_recv.at[1], p) for n, p in enumerate((y_up, y_down))]

    def w2_copies():
        return [remote(w2.at[0, n], w2.at[1, n], sent.at[2], w_recv.at[2], p) for n, p in enumerate((y_up, y_down))]

    def wide_one(g):
        wx_copy().wait_recv()
        across = wide_block(lax.rem(y + 2, 4)).astype(BF16)
        w1[0, 0] = across[:, :part]
        w1[0, 1] = across[:, part:]
        for copy in w1_copies():
            copy.start()

    def wide_two(g):
        up = wide_block(lax.rem(y + 1, 4))
        down = wide_block(lax.rem(y + 3, 4))
        arrived(w_recv.at[1], w1.at[1])
        w2[0, 0, :, :part] = (up[:, :part] + w1[1, 0].astype(F32)).astype(BF16)
        w2[0, 0, :, part:] = up[:, part:].astype(BF16)
        w2[0, 1, :, :part] = down[:, :part].astype(BF16)
        w2[0, 1, :, part:] = (down[:, part:] + w1[1, 1].astype(F32)).astype(BF16)
        for copy in w2_copies():
            copy.start()

    share = rows_dev // 2
    own_share = pl.ds(pl.multiple_of(jnp.where(zk == 2, share, 0), share), share)

    def rz_copies(g):
        return [
            remote(
                dz.at[g, pl.ds(n * share, share)],
                rz.at[g, zk - jnp.where(zk > n + 1, 1, 0)],
                sent.at[4],
                rz_recv.at[g],
                owners[n],
            )
            for n in range(2)
        ]

    def reduce_z(g):
        at = slice(g * cols, (g + 1) * cols)
        if g == WIDE:
            arrived(w_recv.at[2], w2.at[1])
            total = wide_block(y) + w2[1, 0].astype(F32) + w2[1, 1].astype(F32)
        else:
            rx_copy(g).wait_recv()
            rows = block_rows(xl)
            total = own[g, rows, :] + r2[g, 0, rows, :].astype(F32) + r2[g, 1, rows, :].astype(F32)
            total += rx[g].astype(F32)
        drift = (av[:, at] - wv[2, :rows_dev, at].astype(F32)) / inner_rate
        dz[g] = (total + drift).astype(BF16)
        for n, copy in enumerate(rz_copies(g)):
            pl.when(zk != n + 1)(copy.start)

    def mix(g):
        @pl.when(inner)
        def _():
            arrived(rz_recv.at[g], rz.at[g])
            at = slice(g * cols, (g + 1) * cols)
            total = dz[g, own_share, :].astype(F32)
            for n in range(3):
                total += rz[g, n].astype(F32)
            mean = (0.25 * total).astype(BF16)
            mz[g] = mean
            mixb[own_share, at] = mean
            for peer in z_peers:
                remote(mz.at[g], mixb.at[own_share, at], sent.at[4], mz_recv.at[g], peer).start()

    def settle(g):
        pl.when(inner)(functools.partial(arrived, mz_recv.at[g], mz.at[g]))
        pl.when(~inner)(functools.partial(arrived, mz_recv.at[g], dz.at[g]))

    loads[6].wait()
    loads[7].wait()

    def scan_core(g):
        return core_copy(both, pl.ds(g, 1), 1, c_recv.at[g])

    def scan_x(g):
        return x_copy(both, pl.ds(g, 1), 1, x_recv.at[g])

    def scan_back(g):
        return back_copy(both, pl.ds(g, 1), 1, b_recv.at[g])

    def y_args(kind, g):
        return (kind, pl.ds(g, 1), y_recv.at[kind - 1, g])

    def state_step(g):
        over(states, g)

    later_seen = set()

    def later_step(g):
        part = min(g, 1)
        if part not in later_seen:
            later_seen.add(part)
            a_back[part].wait_recv()
        over(with_later, g)
        scan_core(g).start()

    def later_states():
        a_x[1].wait_recv()
        back_fill(0, rest)
        a_back[1].start()

    def y_step(g):
        scan_core(g).wait_recv()
        for kind in (1, 2):
            y_send(*y_args(kind, g))

    def x_step(g):
        for kind in (1, 2):
            y_wait(*y_args(kind, g))
            x_fill(kind, pl.ds(g, 1))
        scan_x(g).start()

    def back_step(g):
        scan_x(g).wait_recv()
        for kind in (1, 2):
            back_fill(kind, pl.ds(g, 1))
        scan_back(g).start()

    def grad_step(g):
        scan_back(g).wait_recv()
        grads(g)

    def base_step(g):
        over(bases, g)

    def prepare(g):
        turn_own(1)
        arrived(p_recv.at[1], xp.at[pl.ds(0, 4)])
        turn_theirs(1)

    def know(g):
        @pl.when(zk < 2)
        def _():
            pl.semaphore_wait(low_known, 1)

        @pl.when(zk >= 2)
        def _():
            pl.semaphore_wait(high_known, 1)

    steps = {
        "state": state_step,
        "later": later_step,
        "a_rest": lambda g: later_states(),
        "y": y_step,
        "x": x_step,
        "back": back_step,
        "base": base_step,
        "prepare": prepare,
        "know": know,
        "grad": grad_step,
        "w0": wide_out,
        "wo": wide_own,
        "w1": wide_one,
        "w2": wide_two,
        "r1": reduce_one,
        "sides": sides,
        "r2": reduce_two,
        "own": own_block,
        "rx": reduce_x,
        "rz": reduce_z,
        "mix": mix,
        "end": settle,
    }
    for name, g in ORDER:
        steps[name](g)

    out_ref[...] = mixb[...]

    def drain(sem, ref):
        remote(ref, ref, sent.at[sem], sent.at[sem], core_peer).wait_send()

    drain(0, wv.at[pl.ds(0, 3), pl.ds(0, tokens)])
    drain(1, x2)
    drain(2, vp.at[pl.ds(0, 15 * tokens // 16)])
    unit = tokens // 8
    for n in range(4):
        pl.when(y == n)(functools.partial(drain, 3, vv.at[pl.ds(0, (3 + n) * unit)]))
    pl.when(inner)(functools.partial(drain, 4, vv.at[pl.ds(0, tokens // 2)]))
    pl.when(~inner)(functools.partial(drain, 4, dz))


def mixed_delta(x, q, k, t, w, a, attn_scale, loss_scale):
    tokens, half = x.shape
    width = q.shape[1]
    heads = width // HEAD_DIM
    rows_dev = a.shape[0]
    groups = GROUPS
    per_group = heads // groups
    mine = per_group // 2
    cols = per_group * HEAD_DIM
    two = 2 * rows_dev
    piece = tokens // 2 // CHUNKS
    state = (HEAD_DIM, HEAD_DIM)
    vmem = pltpu.VMEM
    dma = pltpu.SemaphoreType.DMA
    scratch = [
        vmem((2, tokens, half), BF16),
        vmem((8, tokens, HEAD_DIM), BF16),
        vmem((4, 2, rows_dev, 2 * tokens), BF16),
        vmem((2, CHUNKS, piece, half), BF16),
        vmem((tokens, width), BF16),
        vmem((tokens, width), BF16),
        vmem((tokens, width), BF16),
        vmem((3, half, width), BF16),
        vmem((rows_dev, width), F32),
        vmem((heads, HEAD_DIM, tokens), BF16),
        vmem((heads, 2 * HEAD_DIM, tokens), BF16),
        vmem((heads, tokens, tokens), BF16),
        vmem((heads, tokens, tokens), BF16),
        vmem((heads, tokens, 2 * HEAD_DIM), BF16),
        vmem((tokens, width), F32),
        vmem((tokens, width), BF16),
        vmem((heads, tokens, tokens), BF16),
        vmem((heads, *state), F32),
        vmem((tokens, width), F32),
        vmem((3, groups, 2, mine, *state), BF16),
        vmem((3, groups, mine, *state), BF16),
        vmem((3, groups, mine, *state), BF16),
        vmem((3, 3, groups, mine, *state), BF16),
        vmem((3, groups, mine, *state), BF16),
        vmem((3, groups, mine, *state), BF16),
        vmem((3, groups, mine, *state), BF16),
        vmem((3, groups, 2, mine, *state), BF16),
        vmem((groups, 2 * tokens, cols), BF16),
        vmem((groups, 2, two, cols // 2), F32),
        vmem((groups, 2, two, cols // 2), BF16),
        vmem((groups, 2, two, cols // 2), BF16),
        vmem((groups, 2, two, cols), BF16),
        vmem((groups, 2, two, cols), BF16),
        vmem((groups, two, cols), F32),
        vmem((groups, rows_dev, cols), BF16),
        vmem((groups, rows_dev, cols), BF16),
        vmem((groups, rows_dev, cols), BF16),
        vmem((groups, 3, rows_dev // 2, cols), BF16),
        vmem((groups, rows_dev // 2, cols), BF16),
        vmem((rows_dev, width), BF16),
        vmem((heads, *state), F32),
        vmem((2, 4, rows_dev, cols), BF16),
        vmem((4, rows_dev, cols), F32),
        vmem((2, 2, rows_dev, cols // 2), BF16),
        vmem((2, 2, rows_dev, cols), BF16),
        dma((8,)),
        dma((5,)),
        dma((2, CHUNKS)),
        dma((2,)),
        dma((2,)),
        dma((5,)),
        dma((1,)),
        dma((groups,)),
        dma((2, groups)),
        dma((groups,)),
        dma((groups,)),
        dma((groups,)),
        dma((groups,)),
        dma((groups,)),
        dma((groups,)),
        dma((groups,)),
        dma((groups,)),
        dma((3,)),
        pltpu.SemaphoreType.REGULAR,
        pltpu.SemaphoreType.REGULAR,
        pltpu.SemaphoreType.REGULAR,
    ]
    return pl.pallas_call(
        functools.partial(kernel, attn_scale, loss_scale),
        out_shape=pltpu.VMEM((rows_dev, width), BF16),
        in_specs=[pl.BlockSpec(memory_space=pl.ANY)] * 6,
        out_specs=pl.BlockSpec(memory_space=pltpu.VMEM),
        scratch_shapes=scratch,
        compiler_params=pltpu.CompilerParams(
            collective_id=0, has_side_effects=True, vmem_limit_bytes=60 * 1024 * 1024
        ),
    )(x, q, k, t, w, a)


def local(inputs, queries, keys, targets, value_weight, anchor, momentum):
    sequence = queries.shape[1] * lax.axis_size("ctx")
    attn_scale = 1.0 / math.sqrt(HEAD_DIM * sequence)
    loss_scale = 1.0 / math.sqrt(sequence)
    mixed = mixed_delta(
        inputs[0], queries[0], keys[0], targets[0], value_weight[0], anchor, attn_scale, loss_scale
    )
    momentum_next = slow_decay * momentum + mixed.astype(F32)
    anchor_next = anchor - outer_rate * inner_rate * momentum_next
    return (anchor_next[None], momentum_next[None])


def solution(mesh):
    placed = (
        P("rep", "ctx", "head"),
        P("rep", "ctx", "head"),
        P("rep", "ctx", "head"),
        P("rep", "ctx", "head"),
        P("rep", None, "head"),
        P("ctx", "head"),
        P("ctx", "head"),
    )
    return jax.shard_map(
        local,
        mesh=mesh,
        in_specs=placed,
        out_specs=(P("rep", "ctx", "head"), P("rep", "ctx", "head")),
        check_vma=False,
    )
```

```python
import functools
import math

import jax
import jax.numpy as jnp
from jax import lax
from jax.experimental import pallas as pl
from jax.experimental.pallas import tpu as pltpu
from jax.sharding import PartitionSpec as P

HEAD_DIM = 128
GROUPS = 4
WIDE = 2
CHUNKS = 4
MESH = pl.DeviceIdType.MESH

ORDER = (
    ("state", 0), ("later", 0), ("know", 0), ("a_rest", 0), ("state", 2), ("prepare", 0), ("y", 0), ("later", 2),
    ("state", 1), ("later", 1), ("state", 3), ("later", 3), ("y", 2), ("base", 0), ("y", 1), ("base", 3),
    ("y", 3), ("base", 1), ("x", 0), ("base", 2), ("x", 2), ("back", 0), ("x", 1), ("grad", 0),
    ("back", 2), ("x", 3), ("back", 1), ("r1", 0), ("grad", 2), ("own", 0), ("sides", 0), ("back", 3),
    ("grad", 1), ("r2", 0), ("w0", 2), ("grad", 3), ("r1", 1), ("own", 1), ("sides", 1), ("wo", 2),
    ("r1", 3), ("own", 3), ("sides", 3), ("rx", 0), ("r2", 1), ("w1", 2), ("r2", 3), ("rz", 0),
    ("rx", 1), ("w2", 2), ("mix", 0), ("rx", 3), ("rz", 1), ("rz", 2), ("rz", 3), ("end", 0),
    ("mix", 1), ("mix", 2), ("mix", 3), ("end", 1), ("end", 2), ("end", 3),
)

inner_rate = 0.05
slow_decay = 0.5
outer_rate = 1.0

F32 = jnp.float32
BF16 = jnp.bfloat16


def dot(a, b):
    return jnp.dot(a, b, preferred_element_type=F32)


def lanes(index, size=HEAD_DIM):
    return pl.ds(pl.multiple_of(index * size, size), size)


def kernel(
    attn_scale,
    loss_scale,
    x_ref,
    q_ref,
    k_ref,
    t_ref,
    w_ref,
    a_ref,
    out_ref,
    x2,
    xp,
    xt,
    rel,
    qv,
    kv,
    tv,
    wv,
    av,
    qt,
    kq,
    sc,
    sct,
    wqk,
    vp,
    vv,
    ww,
    qtt,
    base,
    st,
    cr,
    tt,
    yr,
    xs,
    xr,
    ps,
    pr,
    gv,
    keep,
    s1,
    r1,
    s2,
    r2,
    own,
    sx,
    rx,
    dz,
    rz,
    mz,
    mixb,
    uu,
    wx,
    wo,
    w1,
    w2,
    load_sem,
    sent,
    f_recv,
    h_recv,
    p_recv,
    a_recv,
    ay_recv,
    c_recv,
    y_recv,
    x_recv,
    b_recv,
    g_recv,
    r1_recv,
    r2_recv,
    r3_recv,
    rx_recv,
    rz_recv,
    mz_recv,
    w_recv,
    y_known,
    low_known,
    high_known,
):
    tokens, width = qv.shape
    half = x2.shape[2]
    heads = width // HEAD_DIM
    per_group = heads // GROUPS
    mine = per_group // 2
    cols = per_group * HEAD_DIM
    rows_dev = av.shape[0]
    gc = loss_scale * attn_scale

    me = lax.axis_index("ctx")
    rep = lax.axis_index("rep")
    head = lax.axis_index("head")
    core = lax.rem(me, 2)
    xl = lax.rem(me // 2, 2)
    y = me // 4
    low = lax.rem(me, 4)
    core_peer = (me + 1 - 2 * core, rep, head)
    x_id = me + 2 - 4 * xl
    x_peer = (x_id, rep, head)
    far_peer = (x_id, rep, 1 - head)
    y_up = (lax.rem(y + 1, 4) * 4 + low, rep, head)
    y_down = (lax.rem(y + 3, 4) * 4 + low, rep, head)
    zk = lax.rem(rep, 4)
    y_far = (lax.rem(y + 2, 4) * 4 + low, rep, head)
    z_up = (me, lax.rem(rep + 1, 8), head)
    z_down = (me, lax.rem(rep + 7, 8), head)
    inner = (zk > 0) & (zk < 3)
    z_peers = [(me, rep - zk + lax.rem(zk + d, 4), head) for d in (1, 2, 3)]
    owners = [(me, rep - zk + z, head) for z in (1, 2)]

    def remote(src, dst, send, recv, peer):
        return pltpu.make_async_remote_copy(
            src_ref=src, dst_ref=dst, send_sem=send, recv_sem=recv, device_id=peer, device_id_type=MESH
        )

    def arrived(sem, ref):
        pltpu.make_async_copy(ref, ref, sem).wait()

    own_rows = pl.ds(pl.multiple_of(head * half, half), half)
    other_rows = pl.ds(pl.multiple_of((1 - head) * half, half), half)
    loads = [
        pltpu.make_async_copy(src, dst, load_sem.at[n])
        for n, (src, dst) in enumerate(
            (
                (q_ref, qv),
                (k_ref, kv),
                (x_ref, x2.at[0]),
                (w_ref.at[own_rows], wv.at[0]),
                (t_ref, tv),
                (w_ref.at[other_rows], wv.at[1]),
                (w_ref.at[pl.ds(pl.multiple_of(me * rows_dev, rows_dev), rows_dev)], wv.at[2, pl.ds(0, rows_dev)]),
                (a_ref, av),
            )
        )
    ]
    for copy in loads:
        copy.start()

    yr[...] = jnp.zeros_like(yr)

    barrier = pltpu.get_barrier_semaphore()
    peers = [core_peer, x_peer, far_peer, y_up, y_down, z_up, z_down]
    for peer in peers:
        pl.semaphore_signal(barrier, inc=1, device_id=peer, device_id_type=MESH)

    pl.semaphore_wait(barrier, len(peers))

    def tell(sem, peer):
        pl.semaphore_signal(sem, inc=1, device_id=peer, device_id_type=MESH)

    piece = tokens // 2 // CHUNKS
    first = []
    for n in range(CHUNKS):
        for side, peer in ((0, x_peer), (1, far_peer)):
            at = side * (tokens // 2) + n * piece
            first.append(
                remote(x_ref.at[pl.ds(at, piece)], rel.at[side, n], sent.at[0], f_recv.at[side, n], peer)
            )
            first[-1].start()
    for n in range(4):
        src = x_ref.at[:, lanes(2 * n + 1 - core)]
        remote(src, xp.at[head * 4 + n], sent.at[0], p_recv.at[0], core_peer).start()

    tell(y_known, y_down)

    @pl.when(inner)
    def _():
        tell(low_known, z_down)
        tell(high_known, z_up)

    def relay(n):
        for side, peer in ((0, far_peer), (1, x_peer)):
            first[2 * n + side].wait_recv()
            at = side * (tokens // 2) + n * piece
            remote(rel.at[side, n], x2.at[1, pl.ds(at, piece)], sent.at[0], h_recv.at[n // 2], peer).start()

    loads[0].wait()
    loads[1].wait()
    mid = tokens // 2

    def scores(h, carry):
        at = lanes(h)
        q = qv[:, at]
        k = kv[:, at]
        q_t = q.T
        k_t = k.T
        qt[h] = q_t
        kq[h, :HEAD_DIM] = k_t
        row = lax.broadcasted_iota(jnp.int32, (mid, mid), 0)
        col = lax.broadcasted_iota(jnp.int32, (mid, mid), 1)
        lower = row >= col
        upper = row <= col
        for n in range(2):
            rows = slice(n * mid, (n + 1) * mid)
            sc[h, rows, rows] = jnp.where(lower, dot(q[rows], k_t[:, rows]), 0.0).astype(BF16)
            sct[h, rows, rows] = jnp.where(upper, dot(k[rows], q_t[:, rows]), 0.0).astype(BF16)
        sc[h, mid:, :mid] = dot(q[mid:], k_t[:, :mid]).astype(BF16)
        sct[h, :mid, mid:] = dot(k[:mid], q_t[:, mid:]).astype(BF16)
        wqk[h, :, HEAD_DIM:] = k
        st[0, h // per_group, lax.rem(h, per_group) // mine, lax.rem(h, mine)] = dot(q_t, q).astype(BF16)
        return carry

    def products(h, carry):
        at = lanes(h)
        q = qv[:, at]
        t = tv[:, at]
        q_t = qt[h]
        wqk[h, :mid, :HEAD_DIM] = (gc * dot(sct[h, :mid, :], q)).astype(BF16)
        wqk[h, mid:, :HEAD_DIM] = (gc * dot(sct[h, mid:, mid:], q[mid:])).astype(BF16)
        kq[h, HEAD_DIM:, :mid] = (gc * dot(q_t, sc[h, :, :mid])).astype(BF16)
        kq[h, HEAD_DIM:, mid:] = (gc * dot(q_t[:, mid:], sc[h, mid:, mid:])).astype(BF16)
        qtt[h] = -loss_scale * dot(q_t, t)
        base[:mid, at] = -loss_scale * dot(sct[h, :mid, :], t)
        base[mid:, at] = -loss_scale * dot(sct[h, mid:, mid:], t[mid:])
        low = dot(sct[h, :mid, mid:], sc[h, mid:, :])
        ww[h, :mid, :mid] = (gc * (low[:, :mid] + dot(sct[h, :mid, :mid], sc[h, :mid, :mid]))).astype(BF16)
        ww[h, :mid, mid:] = (gc * low[:, mid:]).astype(BF16)
        ww[h, mid:, :] = (gc * dot(sct[h, mid:, mid:], sc[h, mid:, :])).astype(BF16)
        return carry

    lax.fori_loop(0, heads, scores, 0)

    both = pl.ds(1, 2)
    alone = pl.ds(0, 1)

    def place(kind):
        return y if kind == 1 else 3 - y

    def core_copy(kinds, g, sem, recv):
        return remote(st.at[kinds, g, 1 - core], cr.at[kinds, g], sent.at[sem], recv, core_peer)

    def y_copies(kind, g, recv):
        ahead, behind = (y_up, y_down) if kind == 1 else (y_down, y_up)
        return [
            remote(tt.at[kind, g], yr.at[kind, d, g], sent.at[3], recv, peer)
            for d, peer in enumerate((ahead, y_far, behind))
        ]

    def y_send(kind, g, recv):
        total = st[kind, g, core].astype(F32) + cr[kind, g].astype(F32)
        tt[kind, g] = total.astype(BF16)
        for d, copy in enumerate(y_copies(kind, g, recv)):
            pl.when(place(kind) < 3 - d)(copy.start)

    def y_wait(kind, g, recv):
        for d in (1, 2, 3):
            pl.when(place(kind) == d)(functools.partial(arrived, recv, yr.at[kind, pl.ds(0, d), g]))

    def earlier(kind, g):
        return yr[kind, 0, g].astype(F32) + yr[kind, 1, g].astype(F32) + yr[kind, 2, g].astype(F32)

    def x_fill(kind, g):
        gives = (xl == 0) if kind == 1 else (xl == 1)
        xs[kind, g] = (earlier(kind, g) + jnp.where(gives, tt[kind, g].astype(F32), 0.0)).astype(BF16)

    def x_copy(kinds, g, sem, recv):
        return remote(xs.at[kinds, g], xr.at[kinds, g], sent.at[sem], recv, x_peer)

    def back_fill(kind, g):
        chip = earlier(kind, g) + xr[kind, g].astype(F32)
        later = (core == 1) if kind == 1 else (core == 0)
        ours = st[kind, g, core].astype(F32)
        theirs = cr[kind, g].astype(F32)
        ps[kind, g] = jnp.where(later, chip, chip + ours).astype(BF16)
        pr[kind, g, core] = jnp.where(later, chip + theirs, chip).astype(BF16)

    def back_copy(kinds, g, sem, recv):
        return remote(ps.at[kinds, g], pr.at[kinds, g, core], sent.at[sem], recv, core_peer)

    every = pl.ds(0, GROUPS)
    head_start = pl.ds(0, 1)
    rest = pl.ds(1, GROUPS - 1)
    a_core = core_copy(alone, every, 2, a_recv.at[0])
    a_x = [x_copy(alone, part, 2, a_recv.at[1 + n]) for n, part in enumerate((head_start, rest))]
    a_back = [back_copy(alone, part, 2, a_recv.at[3 + n]) for n, part in enumerate((head_start, rest))]
    ay = (0, every, ay_recv.at[0])
    a_core.start()

    relay(0)
    a_core.wait_recv()
    pl.semaphore_wait(y_known, 1)
    y_send(*ay)
    relay(1)

    loads[2].wait()
    loads[3].wait()
    wide = 256

    def partial(n, carry):
        at = lanes(n, wide)
        vp[:, at] = dot(x2[0], wv[0, :, at])
        return carry

    lax.fori_loop(0, width // wide, partial, 0)

    loads[4].wait()
    lax.fori_loop(0, 2, products, 0)
    relay(2)
    lax.fori_loop(2, 4, products, 0)
    relay(3)
    y_wait(*ay)
    for copy, which in zip(a_x, (head_start, rest)):
        x_fill(0, which)
        copy.start()
    lax.fori_loop(4, heads, products, 0)

    def turn_own(side):
        def turn(n, carry):
            block = lax.rem(head + side, 2) * 4 + n
            xt[block // 2, lax.rem(block, 2), :, :tokens] = x2[side, :, lanes(2 * n + core)].T
            return carry

        lax.fori_loop(0, 4, turn, 0)

    def turn_theirs(side):
        def turn(n, carry):
            block = lax.rem(head + side, 2) * 4 + n
            xt[block // 2, lax.rem(block, 2), :, tokens:] = xp[block].T
            return carry

        lax.fori_loop(0, 4, turn, 0)

    turn_own(0)
    arrived(p_recv.at[0], xp.at[pl.ds(0, 4)])
    turn_theirs(0)
    loads[5].wait()

    def finish(n):
        size = 2 * piece
        arrived(h_recv.at[n], x2.at[1, pl.ds(0, mid)])
        parts = [slice(side * mid + n * size, side * mid + (n + 1) * size) for side in range(2)]

        def values(m, carry):
            at = lanes(m, wide)
            rows = jnp.concatenate([x2[1, p, :] for p in parts], axis=0)
            got = dot(rows, wv[1, :, at])
            for i, p in enumerate(parts):
                vv[p, at] = (vp[p, at] + got[i * size : (i + 1) * size]).astype(BF16)
            return carry

        tiles = width // wide
        lax.fori_loop(0, tiles // 2, values, 0)
        if n == 1:
            a_x[0].wait_recv()
            back_fill(0, head_start)
            a_back[0].start()
        lax.fori_loop(tiles // 2, tiles, values, 0)

    finish(0)
    finish(1)
    for n in range(4):
        src = x2.at[1, :, lanes(2 * n + 1 - core)]
        remote(src, xp.at[(1 - head) * 4 + n], sent.at[0], p_recv.at[1], core_peer).start()
    def states(h, carry):
        at = lanes(h)
        g, which, n = h // per_group, lax.rem(h, per_group) // mine, lax.rem(h, mine)
        both_states = dot(kq[h], vv[:, at])
        st[1, g, which, n] = both_states[:HEAD_DIM].astype(BF16)
        uu[h] = both_states[HEAD_DIM:] + qtt[h]
        return carry

    def with_later(h, carry):
        g, which, n = h // per_group, lax.rem(h, per_group) // mine, lax.rem(h, mine)
        st[2, g, which, n] = (uu[h] + gc * dot(pr[0, g, which, n], st[1, g, which, n])).astype(BF16)
        return carry

    def bases(h, carry):
        at = lanes(h)
        base[:, at] += dot(ww[h], vv[:, at])
        return carry

    def over(body, g):
        lax.fori_loop(g * per_group, (g + 1) * per_group, body, 0)

    def gv_copy(g):
        return remote(
            gv.at[g, pl.ds(0, tokens)], gv.at[g, pl.ds(tokens, tokens)], sent.at[1], g_recv.at[g], core_peer
        )

    def grads(g):
        def one(n, carry):
            h = g * per_group + n
            at = lanes(h)
            which, i = n // mine, lax.rem(n, mine)
            prefix = pr[1, g, which, i]
            up_to = (prefix.astype(F32) + st[1, g, which, i].astype(F32)).astype(BF16)
            suffix = (gc * dot(pr[0, g, which, i], up_to) + pr[2, g, which, i].astype(F32)).astype(BF16)
            pair = jnp.concatenate([prefix, suffix], axis=0)
            gv[g, :tokens, lanes(n)] = (attn_scale * (base[:, at] + dot(wqk[h], pair))).astype(BF16)
            return carry

        lax.fori_loop(0, per_group, one, 0)
        copy = gv_copy(g)
        copy.start()

    two = 2 * rows_dev
    part = cols // 2

    def block(g, to):
        return dot(xt[to].reshape(two, 2 * tokens), gv[g])

    def strip(g, to):
        return dot(xt[:, to].reshape(4 * rows_dev, 2 * tokens), gv[g]).reshape(4, rows_dev, cols)

    def block_rows(which):
        return pl.ds(pl.multiple_of(which * rows_dev, rows_dev), rows_dev)

    def r1_copies(g):
        return (
            remote(s1.at[g, 0], r1.at[g, 0], sent.at[2], r1_recv.at[g], y_up),
            remote(s1.at[g, 1], r1.at[g, 1], sent.at[2], r1_recv.at[g], y_down),
        )

    def r2_copies(g):
        return [
            remote(s2.at[g, n, rows], r2.at[g, n, rows], sent.at[2], recv.at[g], peer)
            for recv, rows in ((r2_recv, block_rows(1 - xl)), (r3_recv, block_rows(xl)))
            for n, peer in enumerate((y_up, y_down))
        ]

    def reduce_one(g):
        gv_copy(g).wait_recv()
        across = block(g, lax.rem(y + 2, 4)).astype(BF16)
        s1[g, 0] = across[:, :part]
        s1[g, 1] = across[:, part:]
        for copy in r1_copies(g):
            copy.start()

    def sides(g):
        up = block(g, lax.rem(y + 1, 4))
        s2[g, 0, :, part:] = up[:, part:].astype(BF16)
        keep[g, 0] = up[:, :part]
        down = block(g, lax.rem(y + 3, 4))
        s2[g, 1, :, :part] = down[:, :part].astype(BF16)
        keep[g, 1] = down[:, part:]

    def reduce_two(g):
        arrived(r1_recv.at[g], r1.at[g])
        s2[g, 0, :, :part] = (keep[g, 0] + r1[g, 0].astype(F32)).astype(BF16)
        s2[g, 1, :, part:] = (keep[g, 1] + r1[g, 1].astype(F32)).astype(BF16)
        for copy in r2_copies(g):
            copy.start()

    def own_block(g):
        own[g] = block(g, y)

    def rx_copy(g):
        return remote(sx.at[g], rx.at[g], sent.at[2], rx_recv.at[g], x_peer)

    def reduce_x(g):
        arrived(r2_recv.at[g], r2.at[g, 0])
        rows = block_rows(1 - xl)
        sx[g] = (own[g, rows, :] + r2[g, 0, rows, :].astype(F32) + r2[g, 1, rows, :].astype(F32)).astype(BF16)
        copy = rx_copy(g)
        copy.start()

    def wx_copy():
        return remote(wx.at[0], wx.at[1], sent.at[1], w_recv.at[0], x_peer)

    def wide_out(g):
        arrived(g_recv.at[g], gv.at[g, pl.ds(0, tokens)])
        wx[0] = strip(g, 1 - xl).astype(BF16)
        wx_copy().start()

    def wide_own(g):
        wo[...] = strip(g, xl)

    def wide_block(at):
        return wo[at] + wx[1, at].astype(F32)

    def w1_copies():
        return [remote(w1.at[0, n], w1.at[1, n], sent.at[2], w_recv.at[1], p) for n, p in enumerate((y_up, y_down))]

    def w2_copies():
        return [remote(w2.at[0, n], w2.at[1, n], sent.at[2], w_recv.at[2], p) for n, p in enumerate((y_up, y_down))]

    def wide_one(g):
        wx_copy().wait_recv()
        across = wide_block(lax.rem(y + 2, 4)).astype(BF16)
        w1[0, 0] = across[:, :part]
        w1[0, 1] = across[:, part:]
        for copy in w1_copies():
            copy.start()

    def wide_two(g):
        up = wide_block(lax.rem(y + 1, 4))
        down = wide_block(lax.rem(y + 3, 4))
        arrived(w_recv.at[1], w1.at[1])
        w2[0, 0, :, :part] = (up[:, :part] + w1[1, 0].astype(F32)).astype(BF16)
        w2[0, 0, :, part:] = up[:, part:].astype(BF16)
        w2[0, 1, :, :part] = down[:, :part].astype(BF16)
        w2[0, 1, :, part:] = (down[:, part:] + w1[1, 1].astype(F32)).astype(BF16)
        for copy in w2_copies():
            copy.start()

    share = rows_dev // 2
    own_share = pl.ds(pl.multiple_of(jnp.where(zk == 2, share, 0), share), share)

    def rz_copies(g):
        return [
            remote(
                dz.at[g, pl.ds(n * share, share)],
                rz.at[g, zk - jnp.where(zk > n + 1, 1, 0)],
                sent.at[4],
                rz_recv.at[g],
                owners[n],
            )
            for n in range(2)
        ]

    def reduce_z(g):
        at = slice(g * cols, (g + 1) * cols)
        if g == WIDE:
            arrived(w_recv.at[2], w2.at[1])
            total = wide_block(y) + w2[1, 0].astype(F32) + w2[1, 1].astype(F32)
        else:
            arrived(r3_recv.at[g], r2.at[g, 0])
            rx_copy(g).wait_recv()
            rows = block_rows(xl)
            total = own[g, rows, :] + r2[g, 0, rows, :].astype(F32) + r2[g, 1, rows, :].astype(F32)
            total += rx[g].astype(F32)
        drift = (av[:, at] - wv[2, :rows_dev, at].astype(F32)) / inner_rate
        dz[g] = (total + drift).astype(BF16)
        for n, copy in enumerate(rz_copies(g)):
            pl.when(zk != n + 1)(copy.start)

    def mix(g):
        @pl.when(inner)
        def _():
            arrived(rz_recv.at[g], rz.at[g])
            at = slice(g * cols, (g + 1) * cols)
            total = dz[g, own_share, :].astype(F32)
            for n in range(3):
                total += rz[g, n].astype(F32)
            mean = (0.25 * total).astype(BF16)
            mz[g] = mean
            mixb[own_share, at] = mean
            for peer in z_peers:
                remote(mz.at[g], mixb.at[own_share, at], sent.at[4], mz_recv.at[g], peer).start()

    def settle(g):
        pl.when(inner)(functools.partial(arrived, mz_recv.at[g], mz.at[g]))
        pl.when(~inner)(functools.partial(arrived, mz_recv.at[g], dz.at[g]))

    loads[6].wait()
    loads[7].wait()

    def scan_core(g):
        return core_copy(both, pl.ds(g, 1), 1, c_recv.at[g])

    def scan_x(g):
        return x_copy(both, pl.ds(g, 1), 1, x_recv.at[g])

    def scan_back(g):
        return back_copy(both, pl.ds(g, 1), 1, b_recv.at[g])

    def y_args(kind, g):
        return (kind, pl.ds(g, 1), y_recv.at[kind - 1, g])

    def state_step(g):
        over(states, g)

    later_seen = set()

    def later_step(g):
        part = min(g, 1)
        if part not in later_seen:
            later_seen.add(part)
            a_back[part].wait_recv()
        over(with_later, g)
        scan_core(g).start()

    def later_states():
        a_x[1].wait_recv()
        back_fill(0, rest)
        a_back[1].start()

    def y_step(g):
        scan_core(g).wait_recv()
        for kind in (1, 2):
            y_send(*y_args(kind, g))

    def x_step(g):
        for kind in (1, 2):
            y_wait(*y_args(kind, g))
            x_fill(kind, pl.ds(g, 1))
        scan_x(g).start()

    def back_step(g):
        scan_x(g).wait_recv()
        for kind in (1, 2):
            back_fill(kind, pl.ds(g, 1))
        scan_back(g).start()

    def grad_step(g):
        scan_back(g).wait_recv()
        grads(g)

    def base_step(g):
        over(bases, g)

    def prepare(g):
        turn_own(1)
        arrived(p_recv.at[1], xp.at[pl.ds(0, 4)])
        turn_theirs(1)

    def know(g):
        @pl.when(zk < 2)
        def _():
            pl.semaphore_wait(low_known, 1)

        @pl.when(zk >= 2)
        def _():
            pl.semaphore_wait(high_known, 1)

    steps = {
        "state": state_step,
        "later": later_step,
        "a_rest": lambda g: later_states(),
        "y": y_step,
        "x": x_step,
        "back": back_step,
        "base": base_step,
        "prepare": prepare,
        "know": know,
        "grad": grad_step,
        "w0": wide_out,
        "wo": wide_own,
        "w1": wide_one,
        "w2": wide_two,
        "r1": reduce_one,
        "sides": sides,
        "r2": reduce_two,
        "own": own_block,
        "rx": reduce_x,
        "rz": reduce_z,
        "mix": mix,
        "end": settle,
    }
    for name, g in ORDER:
        steps[name](g)

    out_ref[...] = mixb[...]

    def drain(sem, ref):
        remote(ref, ref, sent.at[sem], sent.at[sem], core_peer).wait_send()

    drain(0, wv.at[pl.ds(0, 3), pl.ds(0, tokens)])
    drain(1, x2)
    drain(2, vp.at[pl.ds(0, 15 * tokens // 16)])
    unit = tokens // 8
    for n in range(4):
        pl.when(y == n)(functools.partial(drain, 3, vv.at[pl.ds(0, (3 + n) * unit)]))
    pl.when(inner)(functools.partial(drain, 4, vv.at[pl.ds(0, tokens // 2)]))
    pl.when(~inner)(functools.partial(drain, 4, dz))


def mixed_delta(x, q, k, t, w, a, attn_scale, loss_scale):
    tokens, half = x.shape
    width = q.shape[1]
    heads = width // HEAD_DIM
    rows_dev = a.shape[0]
    groups = GROUPS
    per_group = heads // groups
    mine = per_group // 2
    cols = per_group * HEAD_DIM
    two = 2 * rows_dev
    piece = tokens // 2 // CHUNKS
    state = (HEAD_DIM, HEAD_DIM)
    vmem = pltpu.VMEM
    dma = pltpu.SemaphoreType.DMA
    scratch = [
        vmem((2, tokens, half), BF16),
        vmem((8, tokens, HEAD_DIM), BF16),
        vmem((4, 2, rows_dev, 2 * tokens), BF16),
        vmem((2, CHUNKS, piece, half), BF16),
        vmem((tokens, width), BF16),
        vmem((tokens, width), BF16),
        vmem((tokens, width), BF16),
        vmem((3, half, width), BF16),
        vmem((rows_dev, width), F32),
        vmem((heads, HEAD_DIM, tokens), BF16),
        vmem((heads, 2 * HEAD_DIM, tokens), BF16),
        vmem((heads, tokens, tokens), BF16),
        vmem((heads, tokens, tokens), BF16),
        vmem((heads, tokens, 2 * HEAD_DIM), BF16),
        vmem((tokens, width), F32),
        vmem((tokens, width), BF16),
        vmem((heads, tokens, tokens), BF16),
        vmem((heads, *state), F32),
        vmem((tokens, width), F32),
        vmem((3, groups, 2, mine, *state), BF16),
        vmem((3, groups, mine, *state), BF16),
        vmem((3, groups, mine, *state), BF16),
        vmem((3, 3, groups, mine, *state), BF16),
        vmem((3, groups, mine, *state), BF16),
        vmem((3, groups, mine, *state), BF16),
        vmem((3, groups, mine, *state), BF16),
        vmem((3, groups, 2, mine, *state), BF16),
        vmem((groups, 2 * tokens, cols), BF16),
        vmem((groups, 2, two, cols // 2), F32),
        vmem((groups, 2, two, cols // 2), BF16),
        vmem((groups, 2, two, cols // 2), BF16),
        vmem((groups, 2, two, cols), BF16),
        vmem((groups, 2, two, cols), BF16),
        vmem((groups, two, cols), F32),
        vmem((groups, rows_dev, cols), BF16),
        vmem((groups, rows_dev, cols), BF16),
        vmem((groups, rows_dev, cols), BF16),
        vmem((groups, 3, rows_dev // 2, cols), BF16),
        vmem((groups, rows_dev // 2, cols), BF16),
        vmem((rows_dev, width), BF16),
        vmem((heads, *state), F32),
        vmem((2, 4, rows_dev, cols), BF16),
        vmem((4, rows_dev, cols), F32),
        vmem((2, 2, rows_dev, cols // 2), BF16),
        vmem((2, 2, rows_dev, cols), BF16),
        dma((8,)),
        dma((5,)),
        dma((2, CHUNKS)),
        dma((2,)),
        dma((2,)),
        dma((5,)),
        dma((1,)),
        dma((groups,)),
        dma((2, groups)),
        dma((groups,)),
        dma((groups,)),
        dma((groups,)),
        dma((groups,)),
        dma((groups,)),
        dma((groups,)),
        dma((groups,)),
        dma((groups,)),
        dma((groups,)),
        dma((3,)),
        pltpu.SemaphoreType.REGULAR,
        pltpu.SemaphoreType.REGULAR,
        pltpu.SemaphoreType.REGULAR,
    ]
    return pl.pallas_call(
        functools.partial(kernel, attn_scale, loss_scale),
        out_shape=pltpu.VMEM((rows_dev, width), BF16),
        in_specs=[pl.BlockSpec(memory_space=pl.ANY)] * 6,
        out_specs=pl.BlockSpec(memory_space=pltpu.VMEM),
        scratch_shapes=scratch,
        compiler_params=pltpu.CompilerParams(
            collective_id=0, has_side_effects=True, vmem_limit_bytes=60 * 1024 * 1024
        ),
    )(x, q, k, t, w, a)


def local(inputs, queries, keys, targets, value_weight, anchor, momentum):
    sequence = queries.shape[1] * lax.axis_size("ctx")
    attn_scale = 1.0 / math.sqrt(HEAD_DIM * sequence)
    loss_scale = 1.0 / math.sqrt(sequence)
    mixed = mixed_delta(
        inputs[0], queries[0], keys[0], targets[0], value_weight[0], anchor, attn_scale, loss_scale
    )
    momentum_next = slow_decay * momentum + mixed.astype(F32)
    anchor_next = anchor - outer_rate * inner_rate * momentum_next
    return (anchor_next[None], momentum_next[None])


def solution(mesh):
    placed = (
        P("rep", "ctx", "head"),
        P("rep", "ctx", "head"),
        P("rep", "ctx", "head"),
        P("rep", "ctx", "head"),
        P("rep", None, "head"),
        P("ctx", "head"),
        P("ctx", "head"),
    )
    return jax.shard_map(
        local,
        mesh=mesh,
        in_specs=placed,
        out_specs=(P("rep", "ctx", "head"), P("rep", "ctx", "head")),
        check_vma=False,
    )
```
